256 devices in a mesh: seq: 64 (over z, y, core), tensor: 4 (over x).
Axes of the slice: x: 4, y: 4, z: 8, core: 2. Of those that a mesh axis runs over, the one named last changes fastest.
Arguments:
- tokens: bfloat16 [32768, 2048], P('seq', 'tensor')
- norm_gain: float32 [2048], replicated, may hold values from 0.5 to 1.5
- w_qkv: bfloat16 [2048, 4, 1024], P(None, 'tensor'), may hold values from -0.125 to 0.125
- w_gate_out: bfloat16 [2048, 2048], P(None, 'tensor'), may hold values from -0.125 to 0.125
- gate_down: bfloat16 [2048, 16], replicated
- gate_up: float32 [16, 4, 256], P(None, 'tensor')
- gate_bias: float32 [4, 256], P('tensor')
- conv_weight: float32 [4, 4, 1024], P(None, 'tensor'), may hold values from -3 to 3
- head_gain: float32 [512], replicated, may hold values from 0.5 to 1.5
- w_out: bfloat16 [2048, 2048], P('tensor'), may hold values from -0.125 to 0.125
- spans: int32 [3], replicated, may hold values from 1 to 48, 64 in all
- fills: int32 [3], replicated, may hold values from 1 to 512
- request_prompt: int32 [128], P('seq'), may hold values from -1 to 2, as said below
Outputs:
- mixed: bfloat16 [32768, 2048], P(('seq', 'tensor'))
- owner_state: float32 [128, 4, 256, 512], P('seq', 'tensor')
- owner_edge: bfloat16 [128, 3, 4, 1024], P('seq', None, 'tensor')
The draws below stay inside these ranges and needn't reach their ends.
Inputs may be any that keep to these rules, and one draw needn't show every extreme that they name: `spans`: the prompts lie along seq in order and together cover all its indices. `request_prompt`: slots r * 2 to r * 2 + 1 belong to index r of seq; the first slot of every index names a prompt; every prompt is named by some slot.
All inputs are finite; a program needn't handle non-finite values.
Results may differ from the reference program's by a relative error of at most 0.0095.
Values may be sent and summed in bfloat16 or wider, within the bound.
A program may use at most 128 MiB of HBM per device.

```python
import math
import jax
import jax.numpy as jnp
import numpy as np
from jax import lax

D = 2048
HEADS = 4
DK = 256
DV = 512
RANK = 16
CONV = 4
STRETCH = 64
TOK_DEV = 512
SLOTS = 2
PROMPTS = 3
TOKEN_SLOTS_ALL = 32768
SPAN_MOST = 48
PROMPT_LENGTH_CAP = 24576
REQUESTS = 128
QKVH = 1024
VAL = 2048
N_SEQ = 64
N_TENSOR = 4


def jump_heading(key):
    return jax.random.normal(jax.random.fold_in(key, 101), (D,), jnp.float32)


def draw_tokens(key, part):
    heading_vector = jump_heading(key)
    sudden_jump = jax.random.bernoulli(jax.random.fold_in(key, 12), 2.0 / PROMPT_LENGTH_CAP, (TOKEN_SLOTS_ALL, 1)).astype(jnp.float32)
    random_jitter = jnp.clip(jax.random.normal(jax.random.fold_in(key, 11), (TOKEN_SLOTS_ALL, D), jnp.float32), -6.0, 6.0)
    value_entries = random_jitter + 5.0 * sudden_jump * heading_vector[None, :]
    return value_entries.astype(jnp.bfloat16)


def draw_gate_down(key, part):
    heading_vector = jump_heading(key)
    others = jax.random.normal(jax.random.fold_in(key, 21), (D, RANK), jnp.float32) * D ** (-0.5)
    column = heading_vector / D
    value_entries = jnp.concatenate([column[:, None], others[:, 1:]], axis=1)
    return value_entries.astype(jnp.bfloat16)


def draw_gate_up(key, part):
    leading = -jax.random.uniform(jax.random.fold_in(key, 31), (1, HEADS, DK), jnp.float32, 10.0, 19.0)
    others = jax.random.normal(jax.random.fold_in(key, 32), (RANK - 1, HEADS, DK), jnp.float32) * 0.2
    return jnp.concatenate([leading, others], axis=0)


def draw_gate_bias(key, part):
    share = jax.random.uniform(jax.random.fold_in(key, 41), (HEADS, 1), jnp.float32, 0.1, 0.6)
    coin = jax.random.uniform(jax.random.fold_in(key, 42), (HEADS, DK), jnp.float32)
    fast_rate = jax.random.uniform(jax.random.fold_in(key, 43), (HEADS, DK), jnp.float32, 1.0 / 50.0, 1.0 / 30.0)
    slow_rate = jax.random.uniform(jax.random.fold_in(key, 44), (HEADS, DK), jnp.float32, 0.2, 1.0) / PROMPT_LENGTH_CAP
    rate = jnp.where(coin < share, fast_rate, slow_rate) * 16.0
    return -jnp.log(jnp.expm1(rate))


def draw_fills(key, part):
    value_entries = jax.random.randint(jax.random.fold_in(key, 51), (PROMPTS,), 1, TOK_DEV + 1)
    high_index = jax.random.randint(jax.random.fold_in(key, 52), (), 0, PROMPTS)
    low_index = (high_index + 1 + jax.random.randint(jax.random.fold_in(key, 53), (), 0, max(PROMPTS - 1, 1))) % PROMPTS
    positions = jnp.arange(PROMPTS)
    value_entries = jnp.where(positions == low_index, 1, value_entries)
    value_entries = jnp.where(positions == high_index, TOK_DEV, value_entries)
    return value_entries.astype(jnp.int32)


def draw_request_prompt(key, part):
    devices = REQUESTS // SLOTS
    first_column = jax.random.permutation(jax.random.fold_in(key, 61), jnp.arange(devices, dtype=jnp.int32) % PROMPTS)
    picks = jax.random.randint(jax.random.fold_in(key, 62), (devices,), 0, PROMPTS)
    used = jax.random.randint(jax.random.fold_in(key, 63), (devices,), 0, 2)
    second_column = jnp.where(used > 0, picks, -1)
    return jnp.stack([first_column, second_column], axis=1).reshape(REQUESTS).astype(jnp.int32)


def levels(rng, dims, cuts, low, high):
    def one(position, shards_of):
        draws = jax.random.uniform(jax.random.fold_in(jax.random.fold_in(rng, 6), position), (shards_of,), jnp.float32, low / len(cuts), high / len(cuts))
        return jnp.repeat(jnp.exp(draws), dims[position] // shards_of).reshape((-1,) + (1,) * (len(dims) - position - 1))

    factor_of = one(*cuts[0])
    for cut in cuts[1:]:
        factor_of = factor_of * one(*cut)
    return factor_of


def split_up(number_of, total, limit, skew):
    loads = [(1 << 20) // math.isqrt(standing ** skew) + 1 for standing in range(2, number_of + 1)]
    surplus, given = total - limit - (number_of - 1), [1] * (number_of - 1)
    while surplus > 0:
        movable = [i for i in range(number_of - 1) if given[i] < limit]
        mass, remaining = sum([loads[i] for i in movable]), surplus
        for i in movable:
            extra = min(limit - given[i], max(1, remaining * loads[i] // mass), surplus)
            given[i] = given[i] + extra
            surplus = surplus - extra
    return np.array([limit] + given)


def ragged_sizes(rng, count, total, reach, slope):
    if count == 2:
        one = jax.random.randint(rng, (), max(1, total - reach), min(reach, total - 1) + 1)
        return jnp.stack([one, total - one])
    tallies = jnp.asarray(split_up(count, total, reach, slope), jnp.int32)
    couples = (count - 1) // 2
    donor, taker = tallies[1:1 + 2 * couples:2], tallies[2:2 + 2 * couples:2]
    margin = jnp.minimum(donor - 1, reach - taker)
    shifted = jax.random.randint(jax.random.fold_in(rng, 1), (couples,), 0, 1 << 20) % (margin + 1)
    tallies = tallies.at[1:1 + 2 * couples:2].set(donor - shifted).at[2:2 + 2 * couples:2].set(taker + shifted)
    return tallies[jax.random.permutation(jax.random.fold_in(rng, 2), count)]


def gaussian(own_key, dims, width, limit, shards=(), held_as=jnp.bfloat16):
    drawn = width * jax.random.normal(own_key, dims, jnp.float32)
    if shards:
        drawn = drawn * levels(own_key, dims, shards, -0.22, 0.18)
    return jnp.clip(drawn, -limit, limit).astype(held_as)


def setup_inputs(seed: int = 0) -> dict:
    splits = jax.random.split(jax.random.key(seed), 14)
    tokens = draw_tokens(jax.random.fold_in(splits[13], 71), 0)
    norm_gain = jnp.clip(1.0 + 0.1 * jax.random.normal(splits[1], (D,), jnp.float32), 0.5, 1.5)
    w_qkv = gaussian(splits[2], (D, HEADS, QKVH), D ** -0.5, 0.125, ((1, 4),))
    w_gate_out = gaussian(splits[3], (D, VAL), D ** -0.5, 0.125, ((1, 4),))
    gate_down = draw_gate_down(jax.random.fold_in(splits[13], 71), 0)
    gate_up = draw_gate_up(jax.random.fold_in(splits[13], 71), 0)
    gate_bias = draw_gate_bias(jax.random.fold_in(splits[13], 71), 0)
    conv_weight = gaussian(splits[7], (CONV, HEADS, QKVH), 0.5, 3.0, ((1, 4),), jnp.float32)
    head_gain = jnp.clip(1.0 + 0.1 * jax.random.normal(splits[8], (DV,), jnp.float32), 0.5, 1.5)
    w_out = gaussian(splits[9], (VAL, D), VAL ** -0.5, 0.125, ((0, 4),))
    spans = ragged_sizes(splits[10], PROMPTS, N_SEQ, SPAN_MOST, 2).astype(jnp.int32)
    fills = draw_fills(jax.random.fold_in(splits[13], 71), 0)
    request_prompt = draw_request_prompt(jax.random.fold_in(splits[13], 71), 0)
    return dict(tokens=tokens, norm_gain=norm_gain, w_qkv=w_qkv, w_gate_out=w_gate_out, gate_down=gate_down, gate_up=gate_up, gate_bias=gate_bias, conv_weight=conv_weight, head_gain=head_gain, w_out=w_out, spans=spans, fills=fills, request_prompt=request_prompt)


EPS_IN = 1e-06
EPS_HEAD = 1e-05
EXACT_MATMUL = lax.Precision.HIGHEST

def to_half(array):
    return lax.optimization_barrier(array.astype(jnp.bfloat16)).astype(jnp.float32)

def block_pass(passed_along_state, pieces):
    q_blk, k_blk, value_block, decay_blk = pieces
    k_wide = k_blk.astype(jnp.float32)
    value_wide_rows = value_block.astype(jnp.float32)
    cumulative = jnp.cumsum(decay_blk, axis=0)
    query_decayed = to_half(q_blk * jnp.exp(cumulative))
    state_lookup = to_half(passed_along_state)
    cross_block_term = jnp.einsum('ews,wsp->ewp', query_decayed, state_lookup, precision=EXACT_MATMUL)
    pair_decay = jnp.exp(jnp.minimum(cumulative[:, None] - cumulative[None, :], 0.0))
    causal_mask = jnp.arange(STRETCH)[:, None] >= jnp.arange(STRETCH)[None, :]
    scores = jnp.einsum('ihk,jhk,ijhk->hij', q_blk, k_wide, pair_decay, precision=EXACT_MATMUL)
    scores = to_half(jnp.where(causal_mask[None], scores, 0.0))
    intra_term = jnp.einsum('hij,jhv->ihv', scores, value_wide_rows, precision=EXACT_MATMUL)
    closing_decay = cumulative[-1]
    weight_applied = to_half(k_wide * jnp.exp(closing_decay[None] - cumulative))
    passed_along_state = jnp.exp(closing_decay)[:, :, None] * passed_along_state + jnp.einsum('qbr,qbp->brp', weight_applied, value_wide_rows, precision=EXACT_MATMUL)
    return (passed_along_state, cross_block_term + intra_term)

def into_blocks(array):
    return array.reshape(TOK_DEV // STRETCH, STRETCH, HEADS, array.shape[-1])

def reference(tokens, norm_gain, w_qkv, w_gate_out, gate_down, gate_up, gate_bias, conv_weight, head_gain, w_out, spans, fills, request_prompt):
    span_ends = jnp.cumsum(spans).astype(jnp.int32)
    starts = (span_ends - spans).astype(jnp.int32)
    devices = jnp.arange(N_SEQ, dtype=jnp.int32)
    owner_prompt = lax.optimization_barrier(jnp.sum((span_ends[None, :] <= devices[:, None]).astype(jnp.int32), axis=1))
    first_dev = starts[owner_prompt]
    last_dev = span_ends[owner_prompt] - 1
    live_counts = jnp.where(devices == last_dev, fills[owner_prompt], TOK_DEV).astype(jnp.int32)
    starting = devices == first_dev
    blocks = tokens.reshape(N_SEQ, TOK_DEV, D)
    width_qkv = 2 * DK + DV
    flat_qkv = w_qkv.reshape(D, HEADS * width_qkv)
    flat_up = gate_up.reshape(RANK, HEADS * DK)
    group = HEADS // N_TENSOR

    def block_step(carry, pieces):
        passed_along_state, tail_rows = carry
        x_blk, start_flag, live_rows = pieces
        passed_along_state = jnp.where(start_flag, jnp.zeros_like(passed_along_state), passed_along_state)
        tail_rows = jnp.where(start_flag, jnp.zeros_like(tail_rows), tail_rows)
        valid = jnp.arange(TOK_DEV, dtype=jnp.int32) < live_rows
        value_entries = x_blk.astype(jnp.float32)
        inverse = lax.rsqrt(lax.optimization_barrier(jnp.mean(value_entries * value_entries, axis=1, keepdims=True)) + EPS_IN)
        normed = (value_entries * inverse * norm_gain[None, :]).astype(jnp.bfloat16)
        projected = jnp.dot(normed, flat_qkv, preferred_element_type=jnp.float32).astype(jnp.bfloat16)
        projected = projected.reshape(TOK_DEV, HEADS, width_qkv)
        gate_rounded = jnp.dot(normed, w_gate_out, preferred_element_type=jnp.float32).astype(jnp.bfloat16)
        gate_rounded = lax.optimization_barrier(gate_rounded)
        gate_values = gate_rounded.astype(jnp.float32).reshape(TOK_DEV, HEADS, DV)
        low_rank = jnp.dot(normed, gate_down, preferred_element_type=jnp.float32)
        logits = jnp.dot(low_rank, flat_up, precision=EXACT_MATMUL).reshape(TOK_DEV, HEADS, DK) + gate_bias[None]
        log_decay = jnp.where(valid[:, None, None], jax.nn.log_sigmoid(logits) / 16.0, 0.0)
        extended = jnp.concatenate([tail_rows, projected], axis=0)
        conv_sum = jnp.zeros((TOK_DEV, HEADS, width_qkv), jnp.float32)
        for offset in range(CONV):
            conv_sum = conv_sum + conv_weight[offset][None] * extended[offset:offset + TOK_DEV].astype(jnp.float32)
        activated = jax.nn.silu(conv_sum).astype(jnp.bfloat16)
        query_rows = activated[:, :, :DK].astype(jnp.float32) * DK ** (-0.5)
        key_rows = jnp.where(valid[:, None, None], activated[:, :, DK:2 * DK], jnp.zeros((), jnp.bfloat16))
        value_rows = activated[:, :, 2 * DK:]
        passed_along_state, outputs = lax.scan(block_pass, passed_along_state, (into_blocks(query_rows), into_blocks(key_rows), into_blocks(value_rows), into_blocks(log_decay)))
        attended = outputs.reshape(TOK_DEV, HEADS, DV)
        mean_square = lax.optimization_barrier(jnp.mean(attended * attended, axis=2, keepdims=True))
        gated = (attended * lax.rsqrt(mean_square + EPS_HEAD) * head_gain[None, None, :] * jax.nn.silu(gate_values)).astype(jnp.bfloat16)
        total = jnp.zeros((TOK_DEV, D), jnp.float32)
        for member in range(N_TENSOR):
            group_rows = gated[:, member * group:(member + 1) * group].reshape(TOK_DEV, group * DV)
            group_weights = w_out[member * group * DV:(member + 1) * group * DV]
            rounded = jnp.dot(group_rows, group_weights, preferred_element_type=jnp.float32).astype(jnp.bfloat16)
            rounded = lax.optimization_barrier(rounded)
            total = total + rounded.astype(jnp.float32)
        mixed_blk = jnp.where(valid[:, None], total, 0.0).astype(jnp.bfloat16)
        edge_rows = lax.dynamic_slice_in_dim(extended, live_rows.astype(jnp.int32), CONV - 1, 0)
        return ((passed_along_state, projected[TOK_DEV - CONV + 1:]), (mixed_blk, passed_along_state, edge_rows))
    initial = (jnp.zeros((HEADS, DK, DV), jnp.float32), jnp.zeros((CONV - 1, HEADS, width_qkv), jnp.bfloat16))
    _, (mixed_blocks, end_states, edges) = lax.scan(block_step, initial, (blocks, starting, live_counts))
    mixed = mixed_blocks.reshape(TOKEN_SLOTS_ALL, D)
    closing = (span_ends - 1).astype(jnp.int32)
    prompt_states = end_states[closing]
    prompt_edges = edges[closing]
    live_slot = request_prompt >= 0
    chosen = jnp.maximum(request_prompt, 0).astype(jnp.int32)
    owner_state = jnp.where(live_slot[:, None, None, None], prompt_states[chosen], 0.0)
    owner_edge = jnp.where(live_slot[:, None, None, None], prompt_edges[chosen], jnp.zeros((), jnp.bfloat16))
    return (mixed, owner_state, owner_edge)
```

```python
import functools

import jax
import jax.numpy as jnp
from jax import lax
from jax.experimental import pallas as pl
from jax.experimental.pallas import tpu as pltpu
from jax.sharding import PartitionSpec as P

STRETCH = 64


EPS_IN = 1e-06
EPS_HEAD = 1e-05
EXACT_MATMUL = lax.Precision.HIGHEST
MESH = pl.DeviceIdType.MESH


def from_behind(array, axis, by):
    peers = lax.axis_size(axis)
    pairs = [(i, i + by) for i in range(peers) if 0 <= i + by < peers]
    return lax.ppermute(array, axis, pairs)


def handoff_kernel(
    n,
    rows,
    start_ref,
    end_ref,
    state_ref,
    message_ref,
    incoming_ref,
    owned_ref,
    parts,
    messages,
    back,
    handed,
    incoming,
    owned,
    send_part,
    recv_part,
    send_message,
    recv_message,
    send_back,
    recv_back,
    send_handed,
    recv_handed,
):
    me = lax.axis_index("seq")
    lane_blocks = state_ref.shape[1] // 128

    def block_of(index):
        return (
            pl.ds(pl.multiple_of((index // lane_blocks) * rows, rows), rows),
            pl.ds(pl.multiple_of((index % lane_blocks) * 128, 128), 128),
        )

    barrier = pltpu.get_barrier_semaphore()

    def greet(step, _):
        peer = lax.rem(me + step, n)
        pl.semaphore_signal(barrier, inc=1, device_id={"seq": peer}, device_id_type=MESH)
        return 0

    lax.fori_loop(1, n, greet, 0)
    pl.semaphore_wait(barrier, n - 1)

    my_block = block_of(me)

    def message_to(peer):
        return pltpu.make_async_remote_copy(
            src_ref=message_ref,
            dst_ref=messages.at[me],
            send_sem=send_message.at[peer],
            recv_sem=recv_message.at[me],
            device_id={"seq": peer},
            device_id_type=MESH,
        )

    def part_to(peer):
        return pltpu.make_async_remote_copy(
            src_ref=state_ref.at[block_of(peer)],
            dst_ref=parts.at[me],
            send_sem=send_part.at[peer],
            recv_sem=recv_part.at[me],
            device_id={"seq": peer},
            device_id_type=MESH,
        )

    def back_to(peer):
        return pltpu.make_async_remote_copy(
            src_ref=back.at[peer],
            dst_ref=incoming.at[my_block],
            send_sem=send_back.at[peer],
            recv_sem=recv_back.at[me],
            device_id={"seq": peer},
            device_id_type=MESH,
        )

    def handed_to(peer):
        return pltpu.make_async_remote_copy(
            src_ref=handed.at[peer],
            dst_ref=owned.at[(slice(None),) + my_block],
            send_sem=send_handed.at[peer],
            recv_sem=recv_handed.at[me],
            device_id={"seq": peer},
            device_id_type=MESH,
        )

    def send_first(step, _):
        peer = lax.rem(me + step, n)
        message_to(peer).start()
        part_to(peer).start()
        return 0

    lax.fori_loop(1, n, send_first, 0)
    parts[me] = state_ref[my_block]
    messages[me] = message_ref[...]

    def arrived(make, ref_of, sem):
        def wait(step, _):
            peer = lax.rem(me + step, n)
            ref = ref_of(peer)
            pltpu.make_async_copy(ref, ref, sem.at[peer]).wait()
            return 0

        lax.fori_loop(1, n, wait, 0)

    arrived(None, lambda peer: messages.at[peer], recv_message)
    arrived(None, lambda peer: parts.at[peer], recv_part)

    key_row = (me // lane_blocks) * rows
    lanes = lax.broadcasted_iota(jnp.int32, (rows, 128), 1)
    sublanes = lax.broadcasted_iota(jnp.int32, (rows, 128), 0)
    offset = key_row % 128 + sublanes
    key_lanes = pl.ds(pl.multiple_of((key_row // 128) * 128, 128), 128)
    zero = jnp.zeros((rows, 128), jnp.float32)

    def scan(index, carry):
        running, finals = carry
        running = jnp.where(start_ref[index] == 1, zero, running)
        back[index] = running.astype(jnp.bfloat16)

        @pl.when(index != me)
        def _():
            back_to(index).start()

        row = messages[index, :, key_lanes]
        decay = jnp.sum(jnp.where(lanes == offset, row, 0.0), axis=1, keepdims=True)
        running = decay * running + parts[index].astype(jnp.float32)
        ended = end_ref[index]
        finals = tuple(jnp.where(ended == p, running, f) for p, f in enumerate(finals))
        return running, finals

    _, finals = lax.fori_loop(0, n, scan, (zero, (zero, zero, zero)))

    def hand(step, _):
        peer = lax.rem(me + step, n)
        for slot in range(2):
            wanted = messages[peer, :, pl.ds(256 + 128 * slot, 128)]
            picked = zero
            for p, final in enumerate(finals):
                picked = jnp.where(wanted == float(p), final, picked)
            handed[peer, slot] = picked.astype(jnp.bfloat16)

        @pl.when(step > 0)
        def _():
            handed_to(peer).start()

        return 0

    lax.fori_loop(0, n, hand, 0)
    incoming[my_block] = back[me]
    owned[(slice(None),) + my_block] = handed[me]

    arrived(None, lambda peer: incoming.at[block_of(peer)], recv_back)
    incoming_ref[...] = incoming[...]
    arrived(None, lambda peer: owned.at[(slice(None),) + block_of(peer)], recv_handed)
    owned_ref[...] = owned[...].astype(jnp.float32)

    def drain(step, _):
        peer = lax.rem(me + step, n)
        message_to(peer).wait_send()
        part_to(peer).wait_send()
        back_to(peer).wait_send()
        handed_to(peer).wait_send()
        return 0

    lax.fori_loop(1, n, drain, 0)


def handoff(state, decay, wanted, starts_here, ends_here):
    n = lax.axis_size("seq")
    keys, values = state.shape
    rows = keys * (values // 128) // n
    message = jnp.concatenate(
        [decay[None], jnp.broadcast_to(wanted.astype(jnp.float32)[:, None], (2, 128)).reshape(1, 256)],
        axis=1,
    )
    vmem = pl.BlockSpec(memory_space=pltpu.VMEM)
    smem = pl.BlockSpec(memory_space=pltpu.SMEM)
    return pl.pallas_call(
        functools.partial(handoff_kernel, n, rows),
        out_shape=(
            jax.ShapeDtypeStruct((keys, values), jnp.bfloat16),
            jax.ShapeDtypeStruct((2, keys, values), jnp.float32),
        ),
        in_specs=[smem, smem, vmem, vmem],
        out_specs=(vmem, vmem),
        scratch_shapes=[
            pltpu.VMEM((n, rows, 128), jnp.bfloat16),
            pltpu.VMEM((n, 1, 512), jnp.float32),
            pltpu.VMEM((n, rows, 128), jnp.bfloat16),
            pltpu.VMEM((n, 2, rows, 128), jnp.bfloat16),
            pltpu.VMEM((keys, values), jnp.bfloat16),
            pltpu.VMEM((2, keys, values), jnp.bfloat16),
        ]
        + [pltpu.SemaphoreType.DMA((n,))] * 8,
        compiler_params=pltpu.CompilerParams(collective_id=0, has_side_effects=True),
        name="state_handoff",
    )(starts_here, ends_here, state.astype(jnp.bfloat16), message)


def block_pass(carry, pieces):
    passed_along_state, offset = carry
    q_blk, k_blk, value_block, decay_blk = pieces
    block_rows = q_blk.shape[0]
    k_wide = k_blk.astype(jnp.float32)
    cumulative = jnp.cumsum(decay_blk, axis=0)
    query_decayed = (q_blk * jnp.exp(cumulative)).astype(jnp.bfloat16)
    pair_decay = jnp.exp(jnp.minimum(cumulative[:, None] - cumulative[None, :], 0.0))
    causal_mask = jnp.arange(block_rows)[:, None] >= jnp.arange(block_rows)[None, :]
    scores = jnp.einsum("ihk,jhk,ijhk->hij", q_blk, k_wide, pair_decay, precision=EXACT_MATMUL)
    scores = jnp.where(causal_mask[None], scores, 0.0).astype(jnp.bfloat16)
    intra_term = jnp.einsum("hij,jhv->ihv", scores, value_block, preferred_element_type=jnp.float32)
    closing_decay = cumulative[-1]
    weight_applied = (k_wide * jnp.exp(closing_decay[None] - cumulative)).astype(jnp.bfloat16)
    updated = jnp.exp(closing_decay)[:, :, None] * passed_along_state + jnp.einsum(
        "qbr,qbp->brp", weight_applied, value_block, preferred_element_type=jnp.float32
    )
    return (
        (updated, offset + closing_decay),
        (intra_term, passed_along_state, offset, query_decayed),
    )


def body(
    tokens,
    norm_gain,
    w_qkv,
    w_gate_out,
    gate_down,
    gate_up,
    gate_bias,
    conv_weight,
    head_gain,
    w_out,
    spans,
    fills,
    request_prompt,
):
    row_count = tokens.shape[0]
    local_heads = w_qkv.shape[1]
    width_qkv = w_qkv.shape[2]
    key_width = gate_up.shape[2]
    value_width = head_gain.shape[0]
    model_width = norm_gain.shape[0]
    taps = conv_weight.shape[0]
    prompts = spans.shape[0]
    slot_count = request_prompt.shape[0]
    seq_index = lax.axis_index("seq")
    span_ends = jnp.cumsum(spans)
    starts = span_ends - spans
    my_prompt = jnp.sum((span_ends <= seq_index).astype(jnp.int32))
    picked = jnp.arange(prompts, dtype=jnp.int32) == my_prompt
    first_dev = jnp.sum(jnp.where(picked, starts, 0))
    last_dev = jnp.sum(jnp.where(picked, span_ends - 1, 0))
    is_start = seq_index == first_dev
    is_last = seq_index == last_dev
    live_rows = jnp.where(is_last, jnp.sum(jnp.where(picked, fills, 0)), row_count)
    valid = jnp.arange(row_count, dtype=jnp.int32) < live_rows
    value_entries = tokens.astype(jnp.float32)
    squares = lax.psum(jnp.sum(value_entries * value_entries, axis=1), "tensor")
    inverse = lax.rsqrt(squares / model_width + EPS_IN)
    flat_qkv = w_qkv.reshape(model_width, local_heads * width_qkv)
    normed = (
        lax.all_gather(tokens, "tensor", axis=1, tiled=True).astype(jnp.float32)
        * inverse[:, None]
        * norm_gain[None, :]
    ).astype(jnp.bfloat16)
    qkv_sum = jnp.dot(normed, flat_qkv, preferred_element_type=jnp.float32)
    gate_sum = jnp.dot(normed, w_gate_out, preferred_element_type=jnp.float32)
    low_rank = jnp.dot(normed, gate_down, preferred_element_type=jnp.float32)
    projected = qkv_sum.astype(jnp.bfloat16).reshape(row_count, local_heads, width_qkv)
    gate_rounded = lax.optimization_barrier(gate_sum.astype(jnp.bfloat16))
    gate_values = gate_rounded.astype(jnp.float32).reshape(row_count, local_heads, value_width)
    logits = jnp.dot(
        low_rank, gate_up.reshape(gate_up.shape[0], local_heads * key_width), precision=EXACT_MATMUL
    )
    logits = logits.reshape(row_count, local_heads, key_width) + gate_bias[None]
    log_decay = jnp.where(valid[:, None, None], jax.nn.log_sigmoid(logits) / 16.0, 0.0)
    tail_rows = projected[row_count - taps + 1 :]
    previous = from_behind(tail_rows, "seq", 1)
    previous = jnp.where(is_start, jnp.zeros_like(previous), previous)
    extended = jnp.concatenate([previous, projected], axis=0)
    conv_sum = jnp.zeros((row_count, local_heads, width_qkv), jnp.float32)
    for offset in range(taps):
        conv_sum = conv_sum + conv_weight[offset][None] * extended[
            offset : offset + row_count
        ].astype(jnp.float32)
    activated = jax.nn.silu(conv_sum).astype(jnp.bfloat16)
    query_rows = activated[:, :, :key_width].astype(jnp.float32) * key_width ** (-0.5)
    key_rows = jnp.where(
        valid[:, None, None],
        activated[:, :, key_width : 2 * key_width],
        jnp.zeros((), jnp.bfloat16),
    )
    value_rows = activated[:, :, 2 * key_width :]

    def into_blocks(array):
        return array.reshape(row_count // STRETCH, STRETCH, local_heads, array.shape[-1])

    start_carry = (
        jnp.zeros((local_heads, key_width, value_width), jnp.float32),
        jnp.zeros((local_heads, key_width), jnp.float32),
    )
    (local_state, decay_sum), (local_out, block_starts, block_offsets, query_decayed) = lax.scan(
        block_pass,
        start_carry,
        (
            into_blocks(query_rows),
            into_blocks(key_rows),
            into_blocks(value_rows),
            into_blocks(log_decay),
        ),
    )
    devices = jnp.arange(lax.axis_size("seq"), dtype=jnp.int32)
    starts_here = jnp.any(devices[:, None] == starts[None, :], axis=1).astype(jnp.int32)
    ends_here = jnp.sum(
        jnp.where(
            devices[:, None] == span_ends[None, :] - 1,
            jnp.arange(prompts, dtype=jnp.int32)[None, :] + 1,
            0,
        ),
        axis=1,
    ) - 1
    incoming, owner_state = handoff(
        local_state[0], jnp.exp(decay_sum)[0], request_prompt, starts_here, ends_here
    )
    incoming = incoming.astype(jnp.float32)[None]
    owner_state = owner_state[:, None]
    full_starts = block_starts + jnp.exp(block_offsets)[:, :, :, None] * incoming[None]
    cross_block_term = jnp.einsum(
        "bchk,bhkv->bchv",
        query_decayed,
        full_starts.astype(jnp.bfloat16),
        preferred_element_type=jnp.float32,
    )
    attended = (cross_block_term + local_out).reshape(row_count, local_heads, value_width)
    mean_square = jnp.mean(attended * attended, axis=2, keepdims=True)
    gated = (
        attended
        * lax.rsqrt(mean_square + EPS_HEAD)
        * head_gain[None, None, :]
        * jax.nn.silu(gate_values)
    ).astype(jnp.bfloat16)
    gated = gated.reshape(row_count, local_heads * value_width)
    share = row_count // lax.axis_size("tensor")
    summed = lax.psum_scatter(
        jnp.dot(gated, w_out, preferred_element_type=jnp.float32).astype(jnp.bfloat16),
        "tensor",
        scatter_dimension=0,
        tiled=True,
    ).astype(jnp.float32)
    own_rows = lax.axis_index("tensor") * share + jnp.arange(share, dtype=jnp.int32)
    mixed = jnp.where((own_rows < live_rows)[:, None], summed, 0.0).astype(jnp.bfloat16)
    edge_rows = lax.dynamic_slice_in_dim(extended, live_rows, taps - 1, 0)
    ending = (is_last & picked)[:, None, None, None]
    edges = lax.psum(jnp.where(ending, edge_rows[None], jnp.zeros((), jnp.bfloat16)), "seq")
    owner_edge = jnp.zeros((slot_count,) + edge_rows.shape, jnp.bfloat16)
    for p in range(prompts):
        owner_edge = jnp.where((request_prompt == p)[:, None, None, None], edges[p][None], owner_edge)
    return (mixed, owner_state, owner_edge)


def solution(mesh):
    return jax.shard_map(
        body,
        mesh=mesh,
        in_specs=(
            P("seq", "tensor"),
            P(),
            P(None, "tensor", None),
            P(None, "tensor"),
            P(),
            P(None, "tensor", None),
            P("tensor", None),
            P(None, "tensor", None),
            P(),
            P("tensor", None),
            P(),
            P(),
            P("seq"),
        ),
        out_specs=(
            P(("seq", "tensor"), None),
            P("seq", "tensor", None, None),
            P("seq", None, "tensor", None),
        ),
        check_vma=False,
    )
```

```python
import functools

import jax
import jax.numpy as jnp
from jax import lax
from jax.experimental import pallas as pl
from jax.experimental.pallas import tpu as pltpu
from jax.sharding import PartitionSpec as P

STRETCH = 64


EPS_IN = 1e-06
EPS_HEAD = 1e-05
EXACT_MATMUL = lax.Precision.HIGHEST
MESH = pl.DeviceIdType.MESH


def from_behind(array, axis, by):
    peers = lax.axis_size(axis)
    pairs = [(i, i + by) for i in range(peers) if 0 <= i + by < peers]
    return lax.ppermute(array, axis, pairs)


def handoff_kernel(
    n,
    group,
    rows,
    start_ref,
    end_ref,
    state_ref,
    message_ref,
    edge_ref,
    incoming_ref,
    owned_ref,
    owned_edge_ref,
    parts,
    messages,
    back,
    handed,
    incoming,
    owned,
    send_part,
    recv_part,
    send_message,
    recv_message,
    send_back,
    recv_back,
    send_handed,
    recv_handed,
    edges,
    picked_edges,
    owned_edges,
    send_edge,
    recv_edge,
    send_picked,
    recv_picked,
):
    me = lax.axis_index("seq")
    lane_blocks = state_ref.shape[1] // 128

    def block_of(index):
        return (
            pl.ds(pl.multiple_of((index // lane_blocks) * rows, rows), rows),
            pl.ds(pl.multiple_of((index % lane_blocks) * 128, 128), 128),
        )

    barrier = pltpu.get_barrier_semaphore()

    def greet(step, _):
        peer = lax.rem(me + step, n)
        pl.semaphore_signal(barrier, inc=1, device_id={"seq": peer}, device_id_type=MESH)
        return 0

    lax.fori_loop(1, n, greet, 0)
    pl.semaphore_wait(barrier, n - 1)

    my_block = block_of(me)

    def message_to(peer):
        return pltpu.make_async_remote_copy(
            src_ref=message_ref,
            dst_ref=messages.at[me],
            send_sem=send_message.at[peer],
            recv_sem=recv_message.at[me],
            device_id={"seq": peer},
            device_id_type=MESH,
        )

    def part_to(peer):
        return pltpu.make_async_remote_copy(
            src_ref=state_ref.at[block_of(peer)],
            dst_ref=parts.at[me],
            send_sem=send_part.at[peer],
            recv_sem=recv_part.at[me],
            device_id={"seq": peer},
            device_id_type=MESH,
        )

    def back_to(peer):
        return pltpu.make_async_remote_copy(
            src_ref=back.at[peer],
            dst_ref=incoming.at[my_block],
            send_sem=send_back.at[peer],
            recv_sem=recv_back.at[me],
            device_id={"seq": peer},
            device_id_type=MESH,
        )

    def handed_to(peer):
        return pltpu.make_async_remote_copy(
            src_ref=handed.at[peer],
            dst_ref=owned.at[(slice(None),) + my_block],
            send_sem=send_handed.at[peer],
            recv_sem=recv_handed.at[me],
            device_id={"seq": peer},
            device_id_type=MESH,
        )

    first_of_group = (me // group) * group
    member = me % group
    level = me // group
    levels = n // group

    def edge_to(other):
        return pltpu.make_async_remote_copy(
            src_ref=edge_ref,
            dst_ref=edges.at[level],
            send_sem=send_edge.at[other],
            recv_sem=recv_edge.at[level],
            device_id={"seq": other * group + member},
            device_id_type=MESH,
        )

    def picked_to(other):
        return pltpu.make_async_remote_copy(
            src_ref=picked_edges.at[other],
            dst_ref=owned_edges.at[member],
            send_sem=send_picked.at[other],
            recv_sem=recv_picked.at[member],
            device_id={"seq": first_of_group + other},
            device_id_type=MESH,
        )

    def around(count, own, action):
        def run(step, _):
            action(lax.rem(own + step, count))
            return 0

        lax.fori_loop(1, count, run, 0)

    around(levels, level, lambda other: edge_to(other).start())
    edges[level] = edge_ref[...]

    def send_first(step, _):
        peer = lax.rem(me + step, n)
        message_to(peer).start()
        part_to(peer).start()
        return 0

    lax.fori_loop(1, n, send_first, 0)
    parts[me] = state_ref[my_block]
    messages[me] = message_ref[...]

    def arrived(make, ref_of, sem):
        def wait(step, _):
            peer = lax.rem(me + step, n)
            ref = ref_of(peer)
            pltpu.make_async_copy(ref, ref, sem.at[peer]).wait()
            return 0

        lax.fori_loop(1, n, wait, 0)

    arrived(None, lambda peer: messages.at[peer], recv_message)
    around(
        levels,
        level,
        lambda other: pltpu.make_async_copy(
            edges.at[other], edges.at[other], recv_edge.at[other]
        ).wait(),
    )

    def pick_edges(step, _):
        other = lax.rem(member + step, group)
        for slot in range(2):
            wanted = messages[first_of_group + other, :, pl.ds(256 + 128 * slot, 128)]
            picked = jnp.zeros(edge_ref.shape, jnp.float32)
            for upper in range(levels):
                ended = end_ref[upper * group + member].astype(jnp.float32)
                picked = jnp.where(wanted == ended, edges[upper].astype(jnp.float32), picked)
            picked_edges[other, slot] = picked.astype(jnp.bfloat16)

        @pl.when(step > 0)
        def _():
            picked_to(other).start()

        return 0

    lax.fori_loop(0, group, pick_edges, 0)
    owned_edges[member] = picked_edges[member]
    arrived(None, lambda peer: parts.at[peer], recv_part)

    key_row = (me // lane_blocks) * rows
    tall = min(rows, 128)
    lanes = lax.broadcasted_iota(jnp.int32, (tall, 128), 1)
    sublanes = lax.broadcasted_iota(jnp.int32, (tall, 128), 0)
    offset = key_row % 128 + sublanes

    def decay_column(index):
        columns = []
        for part in range(rows // tall):
            first = pl.multiple_of((key_row // 128 + part) * 128, 128)
            row = messages[index, :, pl.ds(first, 128)]
            columns.append(
                jnp.sum(jnp.where(lanes == offset, row, 0.0), axis=1, keepdims=True)
            )
        return columns[0] if len(columns) == 1 else jnp.concatenate(columns, axis=0)

    zero = jnp.zeros((rows, 128), jnp.float32)

    def scan(index, carry):
        running, finals = carry
        running = jnp.where(start_ref[index] == 1, zero, running)
        back[index] = running.astype(jnp.bfloat16)

        @pl.when(index != me)
        def _():
            back_to(index).start()

        decay = decay_column(index)
        running = decay * running + parts[index].astype(jnp.float32)
        ended = end_ref[index]
        finals = tuple(jnp.where(ended == p, running, f) for p, f in enumerate(finals))
        return running, finals

    _, finals = lax.fori_loop(0, n, scan, (zero, (zero, zero, zero)))

    def hand(step, _):
        peer = lax.rem(me + step, n)
        for slot in range(2):
            wanted = messages[peer, :, pl.ds(256 + 128 * slot, 128)]
            picked = zero
            for p, final in enumerate(finals):
                picked = jnp.where(wanted == float(p), final, picked)
            handed[peer, slot] = picked.astype(jnp.bfloat16)

        @pl.when(step > 0)
        def _():
            handed_to(peer).start()

        return 0

    lax.fori_loop(0, n, hand, 0)
    incoming[my_block] = back[me]
    owned[(slice(None),) + my_block] = handed[me]

    arrived(None, lambda peer: incoming.at[block_of(peer)], recv_back)
    incoming_ref[...] = incoming[...]
    arrived(None, lambda peer: owned.at[(slice(None),) + block_of(peer)], recv_handed)
    owned_ref[...] = owned[...].astype(jnp.float32)

    around(
        group,
        member,
        lambda other: pltpu.make_async_copy(
            owned_edges.at[other], owned_edges.at[other], recv_picked.at[other]
        ).wait(),
    )
    total = owned_edges[0].astype(jnp.float32)
    for other in range(1, group):
        total = total + owned_edges[other].astype(jnp.float32)
    owned_edge_ref[...] = total.astype(jnp.bfloat16)
    around(levels, level, lambda other: edge_to(other).wait_send())
    around(group, member, lambda other: picked_to(other).wait_send())

    def drain(step, _):
        peer = lax.rem(me + step, n)
        message_to(peer).wait_send()
        part_to(peer).wait_send()
        back_to(peer).wait_send()
        handed_to(peer).wait_send()
        return 0

    lax.fori_loop(1, n, drain, 0)


def handoff(state, decay, edge, wanted, starts_here, ends_here):
    n = lax.axis_size("seq")
    group = 8 if n % 8 == 0 else n // 2
    keys, values = state.shape
    rows = keys * (values // 128) // n
    message = jnp.concatenate(
        [decay, jnp.broadcast_to(wanted.astype(jnp.float32)[:, None], (2, 128)).reshape(1, 256)],
        axis=1,
    )
    vmem = pl.BlockSpec(memory_space=pltpu.VMEM)
    smem = pl.BlockSpec(memory_space=pltpu.SMEM)
    return pl.pallas_call(
        functools.partial(handoff_kernel, n, group, rows),
        out_shape=(
            jax.ShapeDtypeStruct((keys, values), jnp.bfloat16),
            jax.ShapeDtypeStruct((2, keys, values), jnp.float32),
            jax.ShapeDtypeStruct((2,) + edge.shape, jnp.bfloat16),
        ),
        in_specs=[smem, smem, vmem, vmem, vmem],
        out_specs=(vmem, vmem, vmem),
        scratch_shapes=[
            pltpu.VMEM((n, rows, 128), jnp.bfloat16),
            pltpu.VMEM((n, 1, 512), jnp.float32),
            pltpu.VMEM((n, rows, 128), jnp.bfloat16),
            pltpu.VMEM((n, 2, rows, 128), jnp.bfloat16),
            pltpu.VMEM((keys, values), jnp.bfloat16),
            pltpu.VMEM((2, keys, values), jnp.bfloat16),
        ]
        + [pltpu.SemaphoreType.DMA((n,))] * 8
        + [
            pltpu.VMEM((n // group,) + edge.shape, jnp.bfloat16),
            pltpu.VMEM((group, 2) + edge.shape, jnp.bfloat16),
            pltpu.VMEM((group, 2) + edge.shape, jnp.bfloat16),
            pltpu.SemaphoreType.DMA((n // group,)),
            pltpu.SemaphoreType.DMA((n // group,)),
            pltpu.SemaphoreType.DMA((group,)),
            pltpu.SemaphoreType.DMA((group,)),
        ],
        compiler_params=pltpu.CompilerParams(collective_id=0, has_side_effects=True),
        name="state_handoff",
    )(starts_here, ends_here, state, message, edge)


def local_kernel(
    live_ref,
    projected_ref,
    low_rank_ref,
    gate_up_ref,
    gate_bias_ref,
    conv_ref,
    out_ref,
    query_ref,
    state_ref,
    decay_ref,
    state,
    offset,
):
    rows = out_ref.shape[0]
    keys, values = state.shape
    halo = projected_ref.shape[0] - rows
    taps = conv_ref.shape[0]
    state[...] = jnp.zeros_like(state)
    offset[...] = jnp.zeros_like(offset)
    row_of = lax.broadcasted_iota(jnp.int32, (STRETCH, 1), 0)
    at_row = lax.broadcasted_iota(jnp.int32, (STRETCH, STRETCH), 0)
    at_col = lax.broadcasted_iota(jnp.int32, (STRETCH, STRETCH), 1)
    lower = (at_row >= at_col).astype(jnp.float32)
    ones = jnp.ones((STRETCH, 128), jnp.float32)

    def contract(a, b, dims, precision=None):
        return lax.dot_general(
            a, b, (dims, ((), ())), precision=precision, preferred_element_type=jnp.float32
        )

    def one_block(block, _):
        base = pl.multiple_of(block * STRETCH, STRETCH)
        here = pl.ds(base, STRETCH)
        window = projected_ref[pl.ds(base, STRETCH + halo), :].astype(jnp.float32)
        total = jnp.zeros((STRETCH, window.shape[1]), jnp.float32)
        for tap in range(taps):
            first = halo - taps + 1 + tap
            total = total + conv_ref[tap : tap + 1, :] * window[first : first + STRETCH]
        activated = (total * jax.nn.sigmoid(total)).astype(jnp.bfloat16)
        valid = base + row_of < live_ref[0]
        query = activated[:, :keys].astype(jnp.float32) * keys ** (-0.5)
        key = jnp.where(valid, activated[:, keys : 2 * keys].astype(jnp.float32), 0.0)
        value = activated[:, 2 * keys :]
        logits = contract(
            low_rank_ref[here, :], gate_up_ref[...], ((1,), (0,)), EXACT_MATMUL
        ) + gate_bias_ref[...]
        log_decay = (jnp.minimum(logits, 0.0) - jnp.log1p(jnp.exp(-jnp.abs(logits)))) / 16.0
        log_decay = jnp.where(valid, log_decay, 0.0)
        running = contract(lower, log_decay, ((1,), (0,)), EXACT_MATMUL)
        closing = running[STRETCH - 1 : STRETCH]
        closing_column = contract(log_decay, ones, ((0,), (0,)), EXACT_MATMUL)

        scores = jnp.zeros((STRETCH, STRETCH), jnp.float32)
        half = STRETCH // 2
        while half >= 8:
            pair = 2 * half
            pieces = []
            for first in range(0, STRETCH, pair):
                middle = running[first + half - 1 : first + half]
                pieces.append(jnp.broadcast_to(middle, (pair, keys)))
            middle = pieces[0] if len(pieces) == 1 else jnp.concatenate(pieces, axis=0)
            factor = jnp.exp(-jnp.abs(running - middle))
            second = row_of % pair >= half
            left = jnp.where(second, query * factor, 0.0).astype(jnp.bfloat16)
            right = jnp.where(second, 0.0, key * factor).astype(jnp.bfloat16)
            part = contract(left, right, ((1,), (1,)))
            scores = scores + jnp.where(at_row // pair == at_col // pair, part, 0.0)
            half //= 2
        for shift in range(8):
            if shift:
                moved_key = pltpu.roll(key, shift, 0)
                moved_sum = pltpu.roll(running, shift, 0)
                product = query * moved_key * jnp.exp(jnp.minimum(running - moved_sum, 0.0))
            else:
                product = query * key
            summed = jnp.sum(product, axis=1, keepdims=True)
            chosen = (at_col == at_row - shift) & (at_row % 8 >= shift)
            scores = scores + jnp.where(chosen, summed, 0.0)

        decayed = (query * jnp.exp(running)).astype(jnp.bfloat16)
        weighted = (key * jnp.exp(closing - running)).astype(jnp.bfloat16)
        query_ref[here, :] = (query * jnp.exp(running + offset[...])).astype(jnp.bfloat16)
        before = state[...]
        out_ref[here, :] = contract(
            scores.astype(jnp.bfloat16), value, ((1,), (0,))
        ) + contract(decayed, before.astype(jnp.bfloat16), ((1,), (0,)))
        factor = jnp.exp(closing_column)
        factor = jnp.concatenate([factor] * (values // 128), axis=1)
        state[...] = factor * before + contract(weighted, value, ((0,), (0,)))
        offset[...] = offset[...] + closing
        return 0

    lax.fori_loop(0, rows // STRETCH, one_block, 0)
    state_ref[...] = state[...].astype(jnp.bfloat16)
    decay_ref[...] = jnp.exp(offset[...])


def local_blocks(live_rows, projected, low_rank, gate_up, gate_bias, conv_weight, values):
    rows = low_rank.shape[0]
    keys = gate_up.shape[1]
    vmem = pl.BlockSpec(memory_space=pltpu.VMEM)
    smem = pl.BlockSpec(memory_space=pltpu.SMEM)
    return pl.pallas_call(
        local_kernel,
        out_shape=(
            jax.ShapeDtypeStruct((rows, values), jnp.float32),
            jax.ShapeDtypeStruct((rows, keys), jnp.bfloat16),
            jax.ShapeDtypeStruct((keys, values), jnp.bfloat16),
            jax.ShapeDtypeStruct((1, keys), jnp.float32),
        ),
        in_specs=[smem] + [vmem] * 5,
        out_specs=(vmem,) * 4,
        scratch_shapes=[
            pltpu.VMEM((keys, values), jnp.float32),
            pltpu.VMEM((1, keys), jnp.float32),
        ],
        name="local_blocks",
    )(live_rows.reshape(1), projected, low_rank, gate_up, gate_bias, conv_weight)


def body(
    tokens,
    norm_gain,
    w_qkv,
    w_gate_out,
    gate_down,
    gate_up,
    gate_bias,
    conv_weight,
    head_gain,
    w_out,
    spans,
    fills,
    request_prompt,
):
    row_count = tokens.shape[0]
    local_heads = w_qkv.shape[1]
    width_qkv = w_qkv.shape[2]
    key_width = gate_up.shape[2]
    value_width = head_gain.shape[0]
    model_width = norm_gain.shape[0]
    taps = conv_weight.shape[0]
    prompts = spans.shape[0]
    slot_count = request_prompt.shape[0]
    seq_index = lax.axis_index("seq")
    span_ends = jnp.cumsum(spans)
    starts = span_ends - spans
    my_prompt = jnp.sum((span_ends <= seq_index).astype(jnp.int32))
    picked = jnp.arange(prompts, dtype=jnp.int32) == my_prompt
    first_dev = jnp.sum(jnp.where(picked, starts, 0))
    last_dev = jnp.sum(jnp.where(picked, span_ends - 1, 0))
    is_start = seq_index == first_dev
    is_last = seq_index == last_dev
    live_rows = jnp.where(is_last, jnp.sum(jnp.where(picked, fills, 0)), row_count)
    valid = jnp.arange(row_count, dtype=jnp.int32) < live_rows
    value_entries = tokens.astype(jnp.float32)
    squares = lax.psum(jnp.sum(value_entries * value_entries, axis=1), "tensor")
    inverse = lax.rsqrt(squares / model_width + EPS_IN)
    flat_qkv = w_qkv.reshape(model_width, local_heads * width_qkv)
    normed = (
        lax.all_gather(tokens, "tensor", axis=1, tiled=True).astype(jnp.float32)
        * inverse[:, None]
        * norm_gain[None, :]
    ).astype(jnp.bfloat16)
    qkv_sum = jnp.dot(normed, flat_qkv, preferred_element_type=jnp.float32)
    gate_sum = jnp.dot(normed, w_gate_out, preferred_element_type=jnp.float32)
    low_rank = jnp.dot(normed, gate_down, preferred_element_type=jnp.float32)
    projected = qkv_sum.astype(jnp.bfloat16).reshape(row_count, local_heads, width_qkv)
    gate_rounded = lax.optimization_barrier(gate_sum.astype(jnp.bfloat16))
    gate_values = gate_rounded.astype(jnp.float32).reshape(row_count, local_heads, value_width)
    tail_rows = projected[row_count - taps + 1 :]
    previous = from_behind(tail_rows, "seq", 1)
    previous = jnp.where(is_start, jnp.zeros_like(previous), previous)
    halo = 16
    front = jnp.zeros((halo - taps + 1, width_qkv), jnp.bfloat16)
    extended = jnp.concatenate([front, previous[:, 0], projected[:, 0]], axis=0)
    local_out, query_decayed, local_state, decay = local_blocks(
        live_rows, extended, low_rank, gate_up[:, 0], gate_bias, conv_weight[:, 0], value_width
    )
    edge_rows = lax.dynamic_slice_in_dim(extended, live_rows + halo - taps + 1, taps - 1, 0)
    edge = jnp.pad(edge_rows.reshape(-1, 128), ((0, 8), (0, 0)))
    devices = jnp.arange(lax.axis_size("seq"), dtype=jnp.int32)
    starts_here = jnp.any(devices[:, None] == starts[None, :], axis=1).astype(jnp.int32)
    ends_here = jnp.sum(
        jnp.where(
            devices[:, None] == span_ends[None, :] - 1,
            jnp.arange(prompts, dtype=jnp.int32)[None, :] + 2,
            0,
        ),
        axis=1,
    ) - 2
    incoming, owner_state, owned_edge = handoff(
        local_state, decay, edge, request_prompt, starts_here, ends_here
    )
    owner_state = owner_state[:, None]
    owner_edge = owned_edge[:, : edge.shape[0] - 8].reshape(
        slot_count, taps - 1, local_heads, width_qkv
    )
    attended = local_out + jnp.dot(query_decayed, incoming, preferred_element_type=jnp.float32)
    attended = attended.reshape(row_count, local_heads, value_width)
    mean_square = jnp.mean(attended * attended, axis=2, keepdims=True)
    gated = (
        attended
        * lax.rsqrt(mean_square + EPS_HEAD)
        * head_gain[None, None, :]
        * jax.nn.silu(gate_values)
    ).astype(jnp.bfloat16)
    gated = gated.reshape(row_count, local_heads * value_width)
    share = row_count // lax.axis_size("tensor")
    summed = lax.psum_scatter(
        jnp.dot(gated, w_out, preferred_element_type=jnp.float32).astype(jnp.bfloat16),
        "tensor",
        scatter_dimension=0,
        tiled=True,
    ).astype(jnp.float32)
    own_rows = lax.axis_index("tensor") * share + jnp.arange(share, dtype=jnp.int32)
    mixed = jnp.where((own_rows < live_rows)[:, None], summed, 0.0).astype(jnp.bfloat16)
    return (mixed, owner_state, owner_edge)


def solution(mesh):
    return jax.shard_map(
        body,
        mesh=mesh,
        in_specs=(
            P("seq", "tensor"),
            P(),
            P(None, "tensor", None),
            P(None, "tensor"),
            P(),
            P(None, "tensor", None),
            P("tensor", None),
            P(None, "tensor", None),
            P(),
            P("tensor", None),
            P(),
            P(),
            P("seq"),
        ),
        out_specs=(
            P(("seq", "tensor"), None),
            P("seq", "tensor", None, None),
            P("seq", None, "tensor", None),
        ),
        check_vma=False,
    )
```

```python
import functools

import jax
import jax.numpy as jnp
from jax import lax
from jax.experimental import pallas as pl
from jax.experimental.pallas import tpu as pltpu
from jax.sharding import PartitionSpec as P

STRETCH = 64


EPS_IN = 1e-06
EPS_HEAD = 1e-05
EXACT_MATMUL = lax.Precision.HIGHEST
MESH = pl.DeviceIdType.MESH


HALO = 16
CHUNKS = ((16, 96, 176), (176, 272, 352), (352, 448, 528))


def neighbours():
    n = lax.axis_size("tensor")
    x = lax.axis_index("tensor")
    return x, lax.rem(x + 1, n), lax.rem(x + n - 1, n), lax.rem(x + 2, n)


def project_kernel(
    start_ref,
    tokens_ref,
    gain_ref,
    qkv_hbm,
    gate_hbm,
    down_ref,
    projected_ref,
    gate_ref,
    low_rank_ref,
    gathered,
    normed,
    qkv,
    gate,
    load_sem,
    send_right,
    send_left,
    from_left,
    from_right,
    pass_right,
    pass_left,
    far_left,
    far_right,
    send_halo,
    recv_halo,
):
    n = lax.axis_size("seq")
    peers = lax.axis_size("tensor")
    me = lax.axis_index("seq")
    x, right, left, far = neighbours()
    after, before = lax.rem(me + 1, n), lax.rem(me + n - 1, n)
    width = tokens_ref.shape[1]
    loads = [
        pltpu.make_async_copy(qkv_hbm, qkv, load_sem.at[0]),
        pltpu.make_async_copy(gate_hbm, gate, load_sem.at[1]),
    ]
    for load in loads:
        load.start()

    barrier = pltpu.get_barrier_semaphore()
    for peer in (right, left):
        pl.semaphore_signal(barrier, inc=1, device_id={"tensor": peer}, device_id_type=MESH)
    for peer in range(peers):
        pl.semaphore_signal(
            barrier, inc=1, device_id={"seq": before, "tensor": peer}, device_id_type=MESH
        )
    pl.semaphore_wait(barrier, 2 + peers)

    def own(chunk, to, send, recv):
        first, _, last = CHUNKS[chunk]
        return pltpu.make_async_remote_copy(
            src_ref=tokens_ref.at[pl.ds(first - HALO, last - first)],
            dst_ref=gathered.at[x, pl.ds(first, last - first)],
            send_sem=send.at[chunk],
            recv_sem=recv.at[chunk],
            device_id={"tensor": to},
            device_id_type=MESH,
        )

    def passed(chunk, owner, to, upper, send, recv):
        first, middle, last = CHUNKS[chunk]
        first, last = (middle, last) if upper else (first, middle)
        ref = gathered.at[owner, pl.ds(first, last - first)]
        return pltpu.make_async_remote_copy(
            src_ref=ref,
            dst_ref=ref,
            send_sem=send.at[chunk],
            recv_sem=recv.at[chunk],
            device_id={"tensor": to},
            device_id_type=MESH,
        )

    def landed(owner, first, last, sem):
        ref = gathered.at[owner, pl.ds(first, last - first)]
        pltpu.make_async_copy(ref, ref, sem).wait()

    halos = []
    for peer in range(peers):
        halos.append(
            pltpu.make_async_remote_copy(
                src_ref=tokens_ref.at[pl.ds(tokens_ref.shape[0] - HALO, HALO)],
                dst_ref=gathered.at[x, pl.ds(0, HALO)],
                send_sem=send_halo.at[peer],
                recv_sem=recv_halo.at[x],
                device_id={"seq": after, "tensor": peer},
                device_id_type=MESH,
            )
        )
    count = len(CHUNKS)
    rights = [own(c, right, send_right, from_left) for c in range(count)]
    lefts = [own(c, left, send_left, from_right) for c in range(count)]
    onward_right = [passed(c, left, right, False, pass_right, far_left) for c in range(count)]
    onward_left = [passed(c, right, left, True, pass_left, far_right) for c in range(count)]
    for copy in (rights[0], lefts[0], *halos, rights[1], lefts[1]):
        copy.start()
    gathered[x, pl.ds(HALO, tokens_ref.shape[0])] = tokens_ref[...]

    def compute(chunk):
        first = 0 if chunk == 0 else CHUNKS[chunk][0]
        last = CHUNKS[chunk][2]
        here = pl.ds(first, last - first)
        squares = jnp.zeros((last - first, 1), jnp.float32)
        for owner in range(peers):
            piece = gathered[owner, here].astype(jnp.float32)
            squares = squares + jnp.sum(piece * piece, axis=1, keepdims=True)
        inverse = lax.rsqrt(squares / (width * peers) + EPS_IN)
        for owner in range(peers):
            lanes = pl.ds(owner * width, width)
            piece = gathered[owner, here].astype(jnp.float32)
            normed[:, lanes] = (piece * inverse * gain_ref[:, lanes]).astype(jnp.bfloat16)
        rows = normed[...]
        made = jnp.dot(rows, qkv[...], preferred_element_type=jnp.float32)
        if chunk == 0:
            row_of = lax.broadcasted_iota(jnp.int32, (last - first, 1), 0)
            made = jnp.where((row_of < HALO) & (start_ref[0] == 1), 0.0, made)
        projected_ref[here, :] = made.astype(jnp.bfloat16)
        gate_ref[here, :] = jnp.dot(
            rows, gate[...], preferred_element_type=jnp.float32
        ).astype(jnp.bfloat16)
        low_rank_ref[here, :] = jnp.dot(rows, down_ref[...], preferred_element_type=jnp.float32)

    def arrive_and_compute(chunk):
        first, middle, last = CHUNKS[chunk]
        landed(far, first, middle, far_left.at[chunk])
        landed(far, middle, last, far_right.at[chunk])
        if chunk == 0:
            for load in loads:
                load.wait()
            for peer in range(peers):
                landed(peer, 0, HALO, recv_halo.at[peer])
        compute(chunk)

    for chunk in range(count):
        first, middle, last = CHUNKS[chunk]
        landed(left, first, last, from_left.at[chunk])
        onward_right[chunk].start()
        landed(right, first, last, from_right.at[chunk])
        onward_left[chunk].start()
        if chunk + 2 < count:
            rights[chunk + 2].start()
            lefts[chunk + 2].start()
        if chunk:
            arrive_and_compute(chunk - 1)
    arrive_and_compute(count - 1)
    for copy in (*rights, *lefts, *onward_right, *onward_left, *halos):
        copy.wait_send()


def project(is_start, tokens, norm_gain, w_qkv, w_gate_out, gate_down):
    rows, width = tokens.shape
    vmem = pl.BlockSpec(memory_space=pltpu.VMEM)
    smem = pl.BlockSpec(memory_space=pltpu.SMEM)
    anywhere = pl.BlockSpec(memory_space=pl.ANY)
    peers = lax.axis_size("tensor")
    tall = rows + HALO
    count = len(CHUNKS)
    return pl.pallas_call(
        project_kernel,
        out_shape=(
            jax.ShapeDtypeStruct((tall, w_qkv.shape[1]), jnp.bfloat16),
            jax.ShapeDtypeStruct((tall, w_gate_out.shape[1]), jnp.bfloat16),
            jax.ShapeDtypeStruct((tall, gate_down.shape[1]), jnp.float32),
        ),
        in_specs=[smem, vmem, vmem, anywhere, anywhere, vmem],
        out_specs=(vmem,) * 3,
        scratch_shapes=[
            pltpu.VMEM((peers, tall, width), jnp.bfloat16),
            pltpu.VMEM((tall // count, width * peers), jnp.bfloat16),
            pltpu.VMEM(w_qkv.shape, jnp.bfloat16),
            pltpu.VMEM(w_gate_out.shape, jnp.bfloat16),
            pltpu.SemaphoreType.DMA((2,)),
        ]
        + [pltpu.SemaphoreType.DMA((count,))] * 8
        + [pltpu.SemaphoreType.DMA((peers,))] * 2,
        compiler_params=pltpu.CompilerParams(
            collective_id=1, has_side_effects=True, vmem_limit_bytes=48 * 1024 * 1024
        ),
        name="gather_project",
    )(is_start.reshape(1), tokens, norm_gain.reshape(1, -1), w_qkv, w_gate_out, gate_down)


def handoff_kernel(
    n,
    group,
    rows,
    start_ref,
    end_ref,
    state_ref,
    message_ref,
    edge_ref,
    live_ref,
    head_gain_ref,
    local_hbm,
    query_hbm,
    gate_hbm,
    out_hbm,
    mixed_ref,
    owned_ref,
    owned_edge_ref,
    parts,
    messages,
    back,
    handed,
    incoming,
    owned,
    send_part,
    recv_part,
    send_message,
    recv_message,
    send_back,
    recv_back,
    send_handed,
    recv_handed,
    edges,
    picked_edges,
    owned_edges,
    send_edge,
    recv_edge,
    send_picked,
    recv_picked,
    local,
    query,
    gate,
    w_out,
    to_far,
    to_left,
    to_right,
    relay_right,
    relay_left,
    sum_right,
    sum_left,
    load_sem,
    send_sum,
    recv_relay,
    recv_sum,
):
    me = lax.axis_index("seq")
    lane_blocks = state_ref.shape[1] // 128

    def block_of(index):
        return (
            pl.ds(pl.multiple_of((index // lane_blocks) * rows, rows), rows),
            pl.ds(pl.multiple_of((index % lane_blocks) * 128, 128), 128),
        )

    barrier = pltpu.get_barrier_semaphore()

    def greet(step, _):
        peer = lax.rem(me + step, n)
        pl.semaphore_signal(barrier, inc=1, device_id={"seq": peer}, device_id_type=MESH)
        return 0

    loads = [
        pltpu.make_async_copy(local_hbm, local, load_sem.at[0]),
        pltpu.make_async_copy(query_hbm, query, load_sem.at[1]),
        pltpu.make_async_copy(gate_hbm, gate, load_sem.at[2]),
        pltpu.make_async_copy(out_hbm, w_out, load_sem.at[3]),
    ]
    for load in loads:
        load.start()
    x, right, left, far = neighbours()
    lax.fori_loop(1, n, greet, 0)
    for peer in (right, left):
        pl.semaphore_signal(barrier, inc=1, device_id={"tensor": peer}, device_id_type=MESH)
    pl.semaphore_wait(barrier, n + 1)

    my_block = block_of(me)
    key_row = (me // lane_blocks) * rows
    wide = max(rows, 128)

    def message_to(peer):
        return pltpu.make_async_remote_copy(
            src_ref=message_ref.at[((peer // lane_blocks) * rows) // wide],
            dst_ref=messages.at[me],
            send_sem=send_message.at[peer],
            recv_sem=recv_message.at[me],
            device_id={"seq": peer},
            device_id_type=MESH,
        )

    def part_to(peer):
        return pltpu.make_async_remote_copy(
            src_ref=state_ref.at[block_of(peer)],
            dst_ref=parts.at[me],
            send_sem=send_part.at[peer],
            recv_sem=recv_part.at[me],
            device_id={"seq": peer},
            device_id_type=MESH,
        )

    def back_to(peer):
        return pltpu.make_async_remote_copy(
            src_ref=back.at[peer],
            dst_ref=incoming.at[my_block],
            send_sem=send_back.at[peer],
            recv_sem=recv_back.at[me],
            device_id={"seq": peer},
            device_id_type=MESH,
        )

    def handed_to(peer):
        return pltpu.make_async_remote_copy(
            src_ref=handed.at[peer],
            dst_ref=owned.at[(slice(None),) + my_block],
            send_sem=send_handed.at[peer],
            recv_sem=recv_handed.at[me],
            device_id={"seq": peer},
            device_id_type=MESH,
        )

    first_of_group = (me // group) * group
    member = me % group
    level = me // group
    levels = n // group

    def edge_to(other):
        return pltpu.make_async_remote_copy(
            src_ref=edge_ref,
            dst_ref=edges.at[level],
            send_sem=send_edge.at[other],
            recv_sem=recv_edge.at[level],
            device_id={"seq": other * group + member},
            device_id_type=MESH,
        )

    def picked_to(other):
        return pltpu.make_async_remote_copy(
            src_ref=picked_edges.at[other],
            dst_ref=owned_edges.at[member],
            send_sem=send_picked.at[other],
            recv_sem=recv_picked.at[member],
            device_id={"seq": first_of_group + other},
            device_id_type=MESH,
        )

    def around(count, own, action):
        def run(step, _):
            action(lax.rem(own + step, count))
            return 0

        lax.fori_loop(1, count, run, 0)

    around(levels, level, lambda other: edge_to(other).start())
    edges[level] = edge_ref[...]

    def send_first(step, _):
        peer = lax.rem(me + step, n)
        message_to(peer).start()
        part_to(peer).start()
        return 0

    lax.fori_loop(1, n, send_first, 0)
    parts[me] = state_ref[my_block]
    messages[me] = message_ref[key_row // wide]

    def arrived(make, ref_of, sem):
        def wait(step, _):
            peer = lax.rem(me + step, n)
            ref = ref_of(peer)
            pltpu.make_async_copy(ref, ref, sem.at[peer]).wait()
            return 0

        lax.fori_loop(1, n, wait, 0)

    arrived(None, lambda peer: messages.at[peer], recv_message)
    around(
        levels,
        level,
        lambda other: pltpu.make_async_copy(
            edges.at[other], edges.at[other], recv_edge.at[other]
        ).wait(),
    )

    def pick_edges(step, _):
        other = lax.rem(member + step, group)
        for slot in range(2):
            wanted = messages[first_of_group + other, :, pl.ds(wide + 128 * slot, 128)]
            picked = jnp.zeros(edge_ref.shape, jnp.float32)
            for upper in range(levels):
                ended = end_ref[upper * group + member].astype(jnp.float32)
                picked = jnp.where(wanted == ended, edges[upper].astype(jnp.float32), picked)
            picked_edges[other, slot] = picked.astype(jnp.bfloat16)

        @pl.when(step > 0)
        def _():
            picked_to(other).start()

        return 0

    lax.fori_loop(0, group, pick_edges, 0)
    owned_edges[member] = picked_edges[member]
    arrived(None, lambda peer: parts.at[peer], recv_part)

    tall = min(rows, 128)
    lanes = lax.broadcasted_iota(jnp.int32, (tall, 128), 1)
    sublanes = lax.broadcasted_iota(jnp.int32, (tall, 128), 0)
    offset = key_row % 128 + sublanes

    def decay_column(index):
        columns = []
        for part in range(rows // tall):
            row = messages[index, :, pl.ds(part * 128, 128)]
            columns.append(
                jnp.sum(jnp.where(lanes == offset, row, 0.0), axis=1, keepdims=True)
            )
        return columns[0] if len(columns) == 1 else jnp.concatenate(columns, axis=0)

    zero = jnp.zeros((rows, 128), jnp.float32)

    def scan(index, carry):
        running, finals = carry
        running = jnp.where(start_ref[index] == 1, zero, running)
        back[index] = running.astype(jnp.bfloat16)

        @pl.when(index != me)
        def _():
            back_to(index).start()

        decay = decay_column(index)
        running = decay * running + parts[index].astype(jnp.float32)
        ended = end_ref[index]
        finals = tuple(jnp.where(ended == p, running, f) for p, f in enumerate(finals))
        return running, finals

    _, finals = lax.fori_loop(0, n, scan, (zero, (zero, zero, zero)))

    def hand(step, _):
        peer = lax.rem(me + step, n)
        for slot in range(2):
            wanted = messages[peer, :, pl.ds(wide + 128 * slot, 128)]
            picked = zero
            for p, final in enumerate(finals):
                picked = jnp.where(wanted == float(p), final, picked)
            handed[peer, slot] = picked.astype(jnp.bfloat16)

        @pl.when(step > 0)
        def _():
            handed_to(peer).start()

        return 0

    lax.fori_loop(0, n, hand, 0)
    incoming[my_block] = back[me]
    owned[(slice(None),) + my_block] = handed[me]

    arrived(None, lambda peer: incoming.at[block_of(peer)], recv_back)
    for load in loads:
        load.wait()
    share = mixed_ref.shape[0]
    half = share // 2
    lower, upper = pl.ds(0, half), pl.ds(half, half)

    def partial_of(quarter):
        here = pl.ds(pl.multiple_of(quarter * share, share), share)
        skipped = pl.ds(pl.multiple_of(quarter * share + HALO, HALO), share)
        attended = local[here, :] + jnp.dot(
            query[here, :], incoming[...], preferred_element_type=jnp.float32
        )
        mean_square = jnp.mean(attended * attended, axis=1, keepdims=True)
        gate_values = gate[skipped, :].astype(jnp.float32)
        gated = (
            attended
            * lax.rsqrt(mean_square + EPS_HEAD)
            * head_gain_ref[...]
            * (gate_values * jax.nn.sigmoid(gate_values))
        ).astype(jnp.bfloat16)
        return jnp.dot(gated, w_out[...], preferred_element_type=jnp.float32).astype(jnp.bfloat16)

    def move(src, dst, to, index, recv):
        return pltpu.make_async_remote_copy(
            src_ref=src,
            dst_ref=dst,
            send_sem=send_sum.at[index],
            recv_sem=recv,
            device_id={"tensor": to},
            device_id_type=MESH,
        )

    moves = [
        move(to_far.at[lower], relay_right, left, 0, recv_relay.at[0]),
        move(to_far.at[upper], relay_left, right, 1, recv_relay.at[1]),
        move(to_left.at[upper], sum_right.at[upper], left, 2, recv_sum.at[0]),
        move(to_right.at[lower], sum_left.at[lower], right, 3, recv_sum.at[1]),
        move(to_left.at[lower], sum_right.at[lower], left, 4, recv_sum.at[2]),
        move(to_right.at[upper], sum_left.at[upper], right, 5, recv_sum.at[3]),
    ]
    to_far[...] = partial_of(far)
    moves[0].start()
    moves[1].start()
    to_left[...] = partial_of(left)
    moves[2].start()
    to_right[...] = partial_of(right)
    moves[3].start()
    moves[0].wait_recv()
    to_left[lower, :] = (
        to_left[lower, :].astype(jnp.float32) + relay_right[...].astype(jnp.float32)
    ).astype(jnp.bfloat16)
    moves[4].start()
    moves[1].wait_recv()
    to_right[upper, :] = (
        to_right[upper, :].astype(jnp.float32) + relay_left[...].astype(jnp.float32)
    ).astype(jnp.bfloat16)
    moves[5].start()
    to_far_done = (moves[0], moves[1])
    for copy in to_far_done:
        copy.wait_send()
    to_far[...] = partial_of(x)
    for copy in moves[2:]:
        copy.wait_recv()
    summed = (
        to_far[...].astype(jnp.float32)
        + sum_right[...].astype(jnp.float32)
        + sum_left[...].astype(jnp.float32)
    )
    row_of = x * share + lax.broadcasted_iota(jnp.int32, (share, 1), 0)
    mixed_ref[...] = jnp.where(row_of < live_ref[0], summed, 0.0).astype(jnp.bfloat16)
    for copy in moves[2:]:
        copy.wait_send()
    arrived(None, lambda peer: owned.at[(slice(None),) + block_of(peer)], recv_handed)
    owned_ref[...] = owned[...].astype(jnp.float32)

    around(
        group,
        member,
        lambda other: pltpu.make_async_copy(
            owned_edges.at[other], owned_edges.at[other], recv_picked.at[other]
        ).wait(),
    )
    total = owned_edges[0].astype(jnp.float32)
    for other in range(1, group):
        total = total + owned_edges[other].astype(jnp.float32)
    owned_edge_ref[...] = total.astype(jnp.bfloat16)
    around(levels, level, lambda other: edge_to(other).wait_send())
    around(group, member, lambda other: picked_to(other).wait_send())

    def drain(step, _):
        peer = lax.rem(me + step, n)
        message_to(peer).wait_send()
        part_to(peer).wait_send()
        back_to(peer).wait_send()
        handed_to(peer).wait_send()
        return 0

    lax.fori_loop(1, n, drain, 0)


def handoff(
    state,
    decay,
    edge,
    wanted,
    starts_here,
    ends_here,
    live_rows,
    head_gain,
    local_out,
    query_decayed,
    gate_values,
    w_out,
):
    n = lax.axis_size("seq")
    group = 8 if n % 8 == 0 else n // 2
    keys, values = state.shape
    rows = keys * (values // 128) // n
    share = local_out.shape[0] // lax.axis_size("tensor")
    wide = max(rows, 128)
    pieces = keys // wide
    message = jnp.concatenate(
        [
            decay.reshape(pieces, 1, wide),
            jnp.broadcast_to(
                wanted.astype(jnp.float32)[None, :, None], (pieces, 2, 128)
            ).reshape(pieces, 1, 256),
        ],
        axis=2,
    )
    vmem = pl.BlockSpec(memory_space=pltpu.VMEM)
    smem = pl.BlockSpec(memory_space=pltpu.SMEM)
    return pl.pallas_call(
        functools.partial(handoff_kernel, n, group, rows),
        out_shape=(
            jax.ShapeDtypeStruct((share, w_out.shape[1]), jnp.bfloat16),
            jax.ShapeDtypeStruct((2, keys, values), jnp.float32),
            jax.ShapeDtypeStruct((2,) + edge.shape, jnp.bfloat16),
        ),
        in_specs=[smem, smem, vmem, vmem, vmem, smem, vmem] + [pl.BlockSpec(memory_space=pl.ANY)] * 4,
        out_specs=(vmem, vmem, vmem),
        scratch_shapes=[
            pltpu.VMEM((n, rows, 128), jnp.bfloat16),
            pltpu.VMEM((n, 1, wide + 256), jnp.float32),
            pltpu.VMEM((n, rows, 128), jnp.bfloat16),
            pltpu.VMEM((n, 2, rows, 128), jnp.bfloat16),
            pltpu.VMEM((keys, values), jnp.bfloat16),
            pltpu.VMEM((2, keys, values), jnp.bfloat16),
        ]
        + [pltpu.SemaphoreType.DMA((n,))] * 8
        + [
            pltpu.VMEM((n // group,) + edge.shape, jnp.bfloat16),
            pltpu.VMEM((group, 2) + edge.shape, jnp.bfloat16),
            pltpu.VMEM((group, 2) + edge.shape, jnp.bfloat16),
            pltpu.SemaphoreType.DMA((n // group,)),
            pltpu.SemaphoreType.DMA((n // group,)),
            pltpu.SemaphoreType.DMA((group,)),
            pltpu.SemaphoreType.DMA((group,)),
            pltpu.VMEM(local_out.shape, jnp.float32),
            pltpu.VMEM(query_decayed.shape, jnp.bfloat16),
            pltpu.VMEM(gate_values.shape, jnp.bfloat16),
            pltpu.VMEM(w_out.shape, jnp.bfloat16),
            pltpu.VMEM((share, w_out.shape[1]), jnp.bfloat16),
            pltpu.VMEM((share, w_out.shape[1]), jnp.bfloat16),
            pltpu.VMEM((share, w_out.shape[1]), jnp.bfloat16),
            pltpu.VMEM((share // 2, w_out.shape[1]), jnp.bfloat16),
            pltpu.VMEM((share // 2, w_out.shape[1]), jnp.bfloat16),
            pltpu.VMEM((share, w_out.shape[1]), jnp.bfloat16),
            pltpu.VMEM((share, w_out.shape[1]), jnp.bfloat16),
            pltpu.SemaphoreType.DMA((4,)),
            pltpu.SemaphoreType.DMA((6,)),
            pltpu.SemaphoreType.DMA((2,)),
            pltpu.SemaphoreType.DMA((4,)),
        ],
        compiler_params=pltpu.CompilerParams(
            collective_id=0, has_side_effects=True, vmem_limit_bytes=48 * 1024 * 1024
        ),
        name="state_handoff",
    )(
        starts_here,
        ends_here,
        state,
        message,
        edge,
        live_rows.reshape(1),
        head_gain.reshape(1, -1),
        local_out,
        query_decayed,
        gate_values,
        w_out,
    )


def local_kernel(
    live_ref,
    projected_ref,
    low_rank_ref,
    gate_up_ref,
    gate_bias_ref,
    conv_ref,
    out_ref,
    query_ref,
    state_ref,
    decay_ref,
    state,
    offset,
):
    rows = out_ref.shape[0]
    keys, values = state.shape
    halo = projected_ref.shape[0] - rows
    taps = conv_ref.shape[0]
    state[...] = jnp.zeros_like(state)
    offset[...] = jnp.zeros_like(offset)
    row_of = lax.broadcasted_iota(jnp.int32, (STRETCH, 1), 0)
    at_row = lax.broadcasted_iota(jnp.int32, (STRETCH, STRETCH), 0)
    at_col = lax.broadcasted_iota(jnp.int32, (STRETCH, STRETCH), 1)
    lower = (at_row >= at_col).astype(jnp.float32)
    ones = jnp.ones((STRETCH, 128), jnp.float32)

    def contract(a, b, dims, precision=None):
        return lax.dot_general(
            a, b, (dims, ((), ())), precision=precision, preferred_element_type=jnp.float32
        )

    def one_block(block, _):
        base = pl.multiple_of(block * STRETCH, STRETCH)
        here = pl.ds(base, STRETCH)
        window = projected_ref[pl.ds(base, STRETCH + halo), :].astype(jnp.float32)
        total = jnp.zeros((STRETCH, window.shape[1]), jnp.float32)
        for tap in range(taps):
            first = halo - taps + 1 + tap
            total = total + conv_ref[tap : tap + 1, :] * window[first : first + STRETCH]
        activated = (total * jax.nn.sigmoid(total)).astype(jnp.bfloat16)
        valid = base + row_of < live_ref[0]
        query = activated[:, :keys].astype(jnp.float32) * keys ** (-0.5)
        key = jnp.where(valid, activated[:, keys : 2 * keys].astype(jnp.float32), 0.0)
        value = activated[:, 2 * keys :]
        logits = contract(
            low_rank_ref[pl.ds(base + halo, STRETCH), :], gate_up_ref[...], ((1,), (0,)), EXACT_MATMUL
        ) + gate_bias_ref[...]
        log_decay = (jnp.minimum(logits, 0.0) - jnp.log1p(jnp.exp(-jnp.abs(logits)))) / 16.0
        log_decay = jnp.where(valid, log_decay, 0.0)
        running = contract(lower, log_decay, ((1,), (0,)), EXACT_MATMUL)
        closing = running[STRETCH - 1 : STRETCH]
        closing_column = contract(log_decay, ones, ((0,), (0,)), EXACT_MATMUL)

        scores = jnp.zeros((STRETCH, STRETCH), jnp.float32)
        half = STRETCH // 2
        while half >= 8:
            pair = 2 * half
            pieces = []
            for first in range(0, STRETCH, pair):
                middle = running[first + half - 1 : first + half]
                pieces.append(jnp.broadcast_to(middle, (pair, keys)))
            middle = pieces[0] if len(pieces) == 1 else jnp.concatenate(pieces, axis=0)
            factor = jnp.exp(-jnp.abs(running - middle))
            second = row_of % pair >= half
            left = jnp.where(second, query * factor, 0.0).astype(jnp.bfloat16)
            right = jnp.where(second, 0.0, key * factor).astype(jnp.bfloat16)
            part = contract(left, right, ((1,), (1,)))
            scores = scores + jnp.where(at_row // pair == at_col // pair, part, 0.0)
            half //= 2
        for shift in range(8):
            if shift:
                moved_key = pltpu.roll(key, shift, 0)
                moved_sum = pltpu.roll(running, shift, 0)
                product = query * moved_key * jnp.exp(jnp.minimum(running - moved_sum, 0.0))
            else:
                product = query * key
            summed = jnp.sum(product, axis=1, keepdims=True)
            chosen = (at_col == at_row - shift) & (at_row % 8 >= shift)
            scores = scores + jnp.where(chosen, summed, 0.0)

        decayed = (query * jnp.exp(running)).astype(jnp.bfloat16)
        weighted = (key * jnp.exp(closing - running)).astype(jnp.bfloat16)
        query_ref[here, :] = (query * jnp.exp(running + offset[...])).astype(jnp.bfloat16)
        before = state[...]
        out_ref[here, :] = contract(
            scores.astype(jnp.bfloat16), value, ((1,), (0,))
        ) + contract(decayed, before.astype(jnp.bfloat16), ((1,), (0,)))
        factor = jnp.exp(closing_column)
        factor = jnp.concatenate([factor] * (values // 128), axis=1)
        state[...] = factor * before + contract(weighted, value, ((0,), (0,)))
        offset[...] = offset[...] + closing
        return 0

    lax.fori_loop(0, rows // STRETCH, one_block, 0)
    state_ref[...] = state[...].astype(jnp.bfloat16)
    decay_ref[...] = jnp.exp(offset[...])


def local_blocks(live_rows, projected, low_rank, gate_up, gate_bias, conv_weight, values):
    rows = low_rank.shape[0] - HALO
    keys = gate_up.shape[1]
    vmem = pl.BlockSpec(memory_space=pltpu.VMEM)
    smem = pl.BlockSpec(memory_space=pltpu.SMEM)
    return pl.pallas_call(
        local_kernel,
        out_shape=(
            jax.ShapeDtypeStruct((rows, values), jnp.float32),
            jax.ShapeDtypeStruct((rows, keys), jnp.bfloat16),
            jax.ShapeDtypeStruct((keys, values), jnp.bfloat16),
            jax.ShapeDtypeStruct((1, keys), jnp.float32),
        ),
        in_specs=[smem] + [vmem] * 5,
        out_specs=(vmem,) * 4,
        scratch_shapes=[
            pltpu.VMEM((keys, values), jnp.float32),
            pltpu.VMEM((1, keys), jnp.float32),
        ],
        name="local_blocks",
    )(live_rows.reshape(1), projected, low_rank, gate_up, gate_bias, conv_weight)


def body(
    tokens,
    norm_gain,
    w_qkv,
    w_gate_out,
    gate_down,
    gate_up,
    gate_bias,
    conv_weight,
    head_gain,
    w_out,
    spans,
    fills,
    request_prompt,
):
    row_count = tokens.shape[0]
    local_heads = w_qkv.shape[1]
    width_qkv = w_qkv.shape[2]
    key_width = gate_up.shape[2]
    value_width = head_gain.shape[0]
    model_width = norm_gain.shape[0]
    taps = conv_weight.shape[0]
    prompts = spans.shape[0]
    slot_count = request_prompt.shape[0]
    seq_index = lax.axis_index("seq")
    span_ends = jnp.cumsum(spans)
    starts = span_ends - spans
    my_prompt = jnp.sum((span_ends <= seq_index).astype(jnp.int32))
    picked = jnp.arange(prompts, dtype=jnp.int32) == my_prompt
    first_dev = jnp.sum(jnp.where(picked, starts, 0))
    last_dev = jnp.sum(jnp.where(picked, span_ends - 1, 0))
    is_start = seq_index == first_dev
    is_last = seq_index == last_dev
    live_rows = jnp.where(is_last, jnp.sum(jnp.where(picked, fills, 0)), row_count)
    flat_qkv = w_qkv.reshape(model_width, local_heads * width_qkv)
    extended, gate_values, low_rank = project(
        is_start.astype(jnp.int32), tokens, norm_gain, flat_qkv, w_gate_out, gate_down
    )
    local_out, query_decayed, local_state, decay = local_blocks(
        live_rows, extended, low_rank, gate_up[:, 0], gate_bias, conv_weight[:, 0], value_width
    )
    edge_rows = lax.dynamic_slice_in_dim(extended, live_rows + HALO - taps + 1, taps - 1, 0)
    edge = jnp.pad(edge_rows.reshape(-1, 128), ((0, 8), (0, 0)))
    devices = jnp.arange(lax.axis_size("seq"), dtype=jnp.int32)
    starts_here = jnp.any(devices[:, None] == starts[None, :], axis=1).astype(jnp.int32)
    ends_here = jnp.sum(
        jnp.where(
            devices[:, None] == span_ends[None, :] - 1,
            jnp.arange(prompts, dtype=jnp.int32)[None, :] + 2,
            0,
        ),
        axis=1,
    ) - 2
    mixed, owner_state, owned_edge = handoff(
        local_state,
        decay,
        edge,
        request_prompt,
        starts_here,
        ends_here,
        live_rows,
        head_gain,
        local_out,
        query_decayed,
        gate_values,
        w_out,
    )
    owner_state = owner_state[:, None]
    owner_edge = owned_edge[:, : edge.shape[0] - 8].reshape(
        slot_count, taps - 1, local_heads, width_qkv
    )
    return (mixed, owner_state, owner_edge)


def solution(mesh):
    return jax.shard_map(
        body,
        mesh=mesh,
        in_specs=(
            P("seq", "tensor"),
            P(),
            P(None, "tensor", None),
            P(None, "tensor"),
            P(),
            P(None, "tensor", None),
            P("tensor", None),
            P(None, "tensor", None),
            P(),
            P("tensor", None),
            P(),
            P(),
            P("seq"),
        ),
        out_specs=(
            P(("seq", "tensor"), None),
            P("seq", "tensor", None, None),
            P("seq", None, "tensor", None),
        ),
        check_vma=False,
    )
```

```python
import functools

import jax
import jax.numpy as jnp
from jax import lax
from jax.experimental import pallas as pl
from jax.experimental.pallas import tpu as pltpu
from jax.sharding import PartitionSpec as P

STRETCH = 64


EPS_IN = 1e-06
EPS_HEAD = 1e-05
EXACT_MATMUL = lax.Precision.HIGHEST
MESH = pl.DeviceIdType.MESH


HALO = 16
CHUNKS = ((16, 96, 176), (176, 272, 352), (352, 448, 528))


def neighbours():
    n = lax.axis_size("tensor")
    x = lax.axis_index("tensor")
    return x, lax.rem(x + 1, n), lax.rem(x + n - 1, n), lax.rem(x + 2, n)


def prompt_edges(spans_ref):
    ends = []
    for p in range(spans_ref.shape[0]):
        ends.append(spans_ref[p] + ends[-1] if ends else spans_ref[p])
    return ends


def starts_prompt(index, ends):
    flag = index == 0
    for end in ends[:-1]:
        flag = flag | (index == end)
    return flag


def live_rows_of(index, ends, fills_ref, rows):
    live = rows
    for p, end in enumerate(ends):
        live = jnp.where(index == end - 1, fills_ref[p], live)
    return live


def project_kernel(
    spans_ref,
    tokens_ref,
    gain_hbm,
    qkv_hbm,
    gate_hbm,
    down_hbm,
    projected_ref,
    gate_ref,
    low_rank_ref,
    gathered,
    normed,
    qkv,
    gate,
    gain_ref,
    down_ref,
    load_sem,
    send_right,
    send_left,
    from_left,
    from_right,
    pass_right,
    pass_left,
    far_left,
    far_right,
    send_halo,
    recv_halo,
):
    n = lax.axis_size("seq")
    peers = lax.axis_size("tensor")
    me = lax.axis_index("seq")
    x, right, left, far = neighbours()
    after, before = lax.rem(me + 1, n), lax.rem(me + n - 1, n)
    width = tokens_ref.shape[1]
    loads = [
        pltpu.make_async_copy(qkv_hbm, qkv, load_sem.at[0]),
        pltpu.make_async_copy(gate_hbm, gate, load_sem.at[1]),
        pltpu.make_async_copy(gain_hbm, gain_ref, load_sem.at[2]),
        pltpu.make_async_copy(down_hbm, down_ref, load_sem.at[3]),
        pltpu.make_async_copy(
            tokens_ref, gathered.at[x, pl.ds(HALO, tokens_ref.shape[0])], load_sem.at[4]
        ),
    ]
    for load in loads:
        load.start()

    barrier = pltpu.get_barrier_semaphore()
    for peer in (right, left):
        pl.semaphore_signal(barrier, inc=1, device_id={"tensor": peer}, device_id_type=MESH)
    for peer in range(peers):
        pl.semaphore_signal(
            barrier, inc=1, device_id={"seq": before, "tensor": peer}, device_id_type=MESH
        )
    pl.semaphore_wait(barrier, 2 + peers)

    def own(chunk, to, send, recv):
        first, _, last = CHUNKS[chunk]
        return pltpu.make_async_remote_copy(
            src_ref=tokens_ref.at[pl.ds(first - HALO, last - first)],
            dst_ref=gathered.at[x, pl.ds(first, last - first)],
            send_sem=send.at[chunk],
            recv_sem=recv.at[chunk],
            device_id={"tensor": to},
            device_id_type=MESH,
        )

    def passed(chunk, owner, to, upper, send, recv):
        first, middle, last = CHUNKS[chunk]
        first, last = (middle, last) if upper else (first, middle)
        ref = gathered.at[owner, pl.ds(first, last - first)]
        return pltpu.make_async_remote_copy(
            src_ref=ref,
            dst_ref=ref,
            send_sem=send.at[chunk],
            recv_sem=recv.at[chunk],
            device_id={"tensor": to},
            device_id_type=MESH,
        )

    def landed(owner, first, last, sem):
        ref = gathered.at[owner, pl.ds(first, last - first)]
        pltpu.make_async_copy(ref, ref, sem).wait()

    halos = []
    for peer in range(peers):
        halos.append(
            pltpu.make_async_remote_copy(
                src_ref=tokens_ref.at[pl.ds(tokens_ref.shape[0] - HALO, HALO)],
                dst_ref=gathered.at[x, pl.ds(0, HALO)],
                send_sem=send_halo.at[peer],
                recv_sem=recv_halo.at[x],
                device_id={"seq": after, "tensor": peer},
                device_id_type=MESH,
            )
        )
    count = len(CHUNKS)
    rights = [own(c, right, send_right, from_left) for c in range(count)]
    lefts = [own(c, left, send_left, from_right) for c in range(count)]
    onward_right = [passed(c, left, right, False, pass_right, far_left) for c in range(count)]
    onward_left = [passed(c, right, left, True, pass_left, far_right) for c in range(count)]
    for copy in (rights[0], lefts[0], *halos, rights[1], lefts[1]):
        copy.start()

    def compute(chunk):
        first = 0 if chunk == 0 else CHUNKS[chunk][0]
        last = CHUNKS[chunk][2]
        here = pl.ds(first, last - first)
        squares = jnp.zeros((last - first, 1), jnp.float32)
        for owner in range(peers):
            piece = gathered[owner, here].astype(jnp.float32)
            squares = squares + jnp.sum(piece * piece, axis=1, keepdims=True)
        inverse = lax.rsqrt(squares / (width * peers) + EPS_IN)
        for owner in range(peers):
            lanes = pl.ds(owner * width, width)
            piece = gathered[owner, here].astype(jnp.float32)
            normed[:, lanes] = (piece * inverse * gain_ref[:, lanes]).astype(jnp.bfloat16)
        rows = normed[...]
        made = jnp.dot(rows, qkv[...], preferred_element_type=jnp.float32)
        if chunk == 0:
            row_of = lax.broadcasted_iota(jnp.int32, (last - first, 1), 0)
            made = jnp.where((row_of < HALO) & starts_prompt(me, prompt_edges(spans_ref)), 0.0, made)
        projected_ref[here, :] = made.astype(jnp.bfloat16)
        gate_ref[here, :] = jnp.dot(
            rows, gate[...], preferred_element_type=jnp.float32
        ).astype(jnp.bfloat16)
        low_rank_ref[here, :] = lax.dot_general(
            rows,
            down_ref[...],
            (((1,), (1,)), ((), ())),
            preferred_element_type=jnp.float32,
        )

    def arrive_and_compute(chunk):
        first, middle, last = CHUNKS[chunk]
        landed(far, first, middle, far_left.at[chunk])
        landed(far, middle, last, far_right.at[chunk])
        if chunk == 0:
            for load in loads:
                load.wait()
            for peer in range(peers):
                landed(peer, 0, HALO, recv_halo.at[peer])
        compute(chunk)

    for chunk in range(count):
        first, middle, last = CHUNKS[chunk]
        landed(left, first, last, from_left.at[chunk])
        onward_right[chunk].start()
        landed(right, first, last, from_right.at[chunk])
        onward_left[chunk].start()
        if chunk + 2 < count:
            rights[chunk + 2].start()
            lefts[chunk + 2].start()
        if chunk:
            arrive_and_compute(chunk - 1)
    arrive_and_compute(count - 1)
    for copy in (*rights, *lefts, *onward_right, *onward_left, *halos):
        copy.wait_send()


def project(spans, tokens, norm_gain, w_qkv, w_gate_out, gate_down):
    rows, width = tokens.shape
    vmem = pl.BlockSpec(memory_space=pltpu.VMEM)
    smem = pl.BlockSpec(memory_space=pltpu.SMEM)
    hbm = pl.BlockSpec(memory_space=pltpu.HBM)
    peers = lax.axis_size("tensor")
    tall = rows + HALO
    count = len(CHUNKS)
    return pl.pallas_call(
        project_kernel,
        out_shape=(
            jax.ShapeDtypeStruct((tall, w_qkv.shape[1]), jnp.bfloat16),
            jax.ShapeDtypeStruct((tall, w_gate_out.shape[1]), jnp.bfloat16),
            jax.ShapeDtypeStruct((tall, gate_down.shape[1]), jnp.float32),
        ),
        in_specs=[smem] + [hbm] * 5,
        out_specs=(vmem,) * 3,
        scratch_shapes=[
            pltpu.VMEM((peers, tall, width), jnp.bfloat16),
            pltpu.VMEM((tall // count, width * peers), jnp.bfloat16),
            pltpu.VMEM(w_qkv.shape, jnp.bfloat16),
            pltpu.VMEM(w_gate_out.shape, jnp.bfloat16),
            pltpu.VMEM((1, width * peers), jnp.float32),
            pltpu.VMEM((gate_down.shape[1], width * peers), jnp.bfloat16),
            pltpu.SemaphoreType.DMA((5,)),
        ]
        + [pltpu.SemaphoreType.DMA((count,))] * 8
        + [pltpu.SemaphoreType.DMA((peers,))] * 2,
        compiler_params=pltpu.CompilerParams(
            collective_id=1, has_side_effects=True, vmem_limit_bytes=20 * 1024 * 1024
        ),
        name="gather_project",
    )(
        spans,
        *(
            pltpu.with_memory_space_constraint(array, pltpu.HBM)
            for array in (tokens, norm_gain.reshape(1, -1), w_qkv, w_gate_out, gate_down.T)
        ),
    )


def handoff_kernel(
    n,
    group,
    rows,
    spans_ref,
    fills_ref,
    request_ref,
    state_ref,
    decay_ref,
    edge_ref,
    head_gain_ref,
    local,
    query,
    gate,
    w_out,
    mixed_ref,
    owned_ref,
    owned_edge_ref,
    message,
    parts,
    messages,
    decays,
    back,
    incoming,
    finals,
    all_finals,
    handed,
    owned,
    edges,
    picked_edges,
    owned_edges,
    to_far,
    to_left,
    to_right,
    relay_right,
    relay_left,
    sum_right,
    sum_left,
    send_sem,
    recv_sem,
    send_sum,
    recv_relay,
    recv_sum,
):
    me = lax.axis_index("seq")
    lane_blocks = state_ref.shape[1] // 128
    slots = request_ref.shape[0]
    ends = prompt_edges(spans_ref)
    wide = max(rows, 128)

    def block_of(index):
        return (
            pl.ds(pl.multiple_of(lax.div(index, lane_blocks) * rows, rows), rows),
            pl.ds(pl.multiple_of(lax.rem(index, lane_blocks) * 128, 128), 128),
        )

    my_block = block_of(me)
    key_row = lax.div(me, lane_blocks) * rows
    level, member = lax.div(me, group), lax.rem(me, group)
    levels = n // group
    first_of_group = level * group
    x, right, left, far = neighbours()

    def around(count, own, action):
        inner = max(k for k in range(1, 10) if (count - 1) % k == 0)

        def run(outer, _):
            for k in range(inner):
                action(lax.rem(own + (outer * inner + k + 1), count))
            return 0

        lax.fori_loop(0, (count - 1) // inner, run, 0)

    def greet(peer):
        pl.semaphore_signal(barrier, inc=1, device_id={"seq": peer}, device_id_type=MESH)

    barrier = pltpu.get_barrier_semaphore()
    around(n, me, greet)
    for peer in (right, left):
        pl.semaphore_signal(barrier, inc=1, device_id={"tensor": peer}, device_id_type=MESH)
    for piece in range(message.shape[0]):
        message[piece, :, :wide] = decay_ref[:, piece * wide : (piece + 1) * wide]
        for slot in range(slots):
            wanted = request_ref[slot].astype(jnp.float32)
            message[piece, :, wide + 128 * slot : wide + 128 * (slot + 1)] = jnp.full(
                (1, 128), wanted, jnp.float32
            )
    pl.semaphore_wait(barrier, n + 1)

    def to_seq(src, dst, peer, index):
        return pltpu.make_async_remote_copy(
            src_ref=src,
            dst_ref=dst,
            send_sem=send_sem.at[index],
            recv_sem=recv_sem.at[index],
            device_id={"seq": peer},
            device_id_type=MESH,
        )

    def message_to(peer):
        piece = lax.div(lax.div(peer, lane_blocks) * rows, wide)
        return to_seq(message.at[piece], messages.at[me], peer, 0)

    def part_to(peer):
        return to_seq(state_ref.at[block_of(peer)], parts.at[me], peer, 1)

    def edge_to(other):
        return to_seq(edge_ref, edges.at[level], other * group + member, 2)

    def picked_to(other):
        return to_seq(
            picked_edges.at[other], owned_edges.at[member], first_of_group + other, 3
        )

    def back_to(peer):
        return to_seq(back.at[peer], incoming.at[my_block], peer, 4)

    def finals_to(other):
        return to_seq(finals, all_finals.at[level], other * group + member, 5)

    mine = (
        slice(None),
        slice(None),
        lax.div(member, lane_blocks),
        slice(None),
        pl.ds(pl.multiple_of(lax.rem(member, lane_blocks) * 128, 128), 128),
    )

    def handed_to(other):
        return to_seq(handed.at[other], owned.at[mine], first_of_group + other, 6)

    def whole(ref, count, sem):
        few = ref.at[pl.ds(0, count)]
        pltpu.make_async_copy(few, few, sem).wait()

    def send_first(peer):
        message_to(peer).start()
        part_to(peer).start()

    around(n, me, send_first)
    around(levels, level, lambda other: edge_to(other).start()) if levels > 1 else None
    parts[me] = state_ref[my_block]
    messages[me] = message[lax.div(key_row, wide)]
    edges[level] = edge_ref[...]
    whole(messages, n - 1, recv_sem.at[0])

    tall = min(rows, 128)
    lanes = lax.broadcasted_iota(jnp.int32, (tall, 128), 1)
    offset = lax.rem(key_row, 128) + lax.broadcasted_iota(jnp.int32, (tall, 128), 0)
    zero = jnp.zeros((rows, 128), jnp.float32)
    step = 8 if n % 8 == 0 else n

    def spread(outer, _):
        for k in range(step):
            index = outer * step + k
            for part in range(rows // tall):
                row = messages[index, :, part * 128 : (part + 1) * 128]
                column = jnp.sum(jnp.where(lanes == offset, row, 0.0), axis=1, keepdims=True)
                decays[index, part * tall : (part + 1) * tall, :] = jnp.broadcast_to(
                    column, (tall, 128)
                )
        return 0

    lax.fori_loop(0, n // step, spread, 0)
    whole(parts, n - 1, recv_sem.at[1])

    def scan(outer, carry):
        running, kept = carry
        for k in range(step):
            index = outer * step + k
            running = jnp.where(starts_prompt(index, ends), zero, running)
            back[index] = running.astype(jnp.bfloat16)
            running = decays[index] * running + parts[index].astype(jnp.float32)
            kept = tuple(
                jnp.where(index == end - 1, running, final) for end, final in zip(ends, kept)
            )
        return running, kept

    _, kept = lax.fori_loop(0, n // step, scan, (zero, (zero,) * len(ends)))
    around(n, me, lambda peer: back_to(peer).start())
    for p, final in enumerate(kept):
        finals[p] = final.astype(jnp.bfloat16)
    around(levels, level, lambda other: finals_to(other).start()) if levels > 1 else None
    incoming[my_block] = back[me]
    all_finals[level] = finals[...]

    if levels > 1:
        whole(edges, levels - 1, recv_sem.at[2])
    ending = [jnp.zeros(edge_ref.shape, jnp.float32)] * len(ends)
    for upper in range(levels):
        held = edges[upper].astype(jnp.float32)
        for p, end in enumerate(ends):
            ending[p] = jnp.where(upper * group + member == end - 1, held, ending[p])
    edge_lanes = edge_ref.shape[1] // 128

    def wanted_by(other, slot):
        return messages[first_of_group + other, :, wide + 128 * slot : wide + 128 * (slot + 1)]

    def pick_edges(other):
        for slot in range(slots):
            wanted = jnp.concatenate([wanted_by(other, slot)] * edge_lanes, axis=1)
            picked = jnp.zeros(edge_ref.shape, jnp.float32)
            for p in range(len(ends)):
                picked = jnp.where(wanted == float(p), ending[p], picked)
            picked_edges[other, slot] = picked.astype(jnp.bfloat16)

    def pick_states(other):
        for slot in range(slots):
            wanted = wanted_by(other, slot)
            for upper in range(levels):
                picked = zero
                for p in range(len(ends)):
                    held = all_finals[upper, p].astype(jnp.float32)
                    picked = jnp.where(wanted == float(p), held, picked)
                handed[other, slot, upper] = picked.astype(jnp.bfloat16)

    def hand_edges(hop, _):
        other = lax.rem(member + hop, group)
        pick_edges(other)

        @pl.when(hop > 0)
        def _():
            picked_to(other).start()

        return 0

    lax.fori_loop(0, group, hand_edges, 0)
    owned_edges[member] = picked_edges[member]

    share = mixed_ref.shape[0]
    half = share // 2
    lower, upper_half = pl.ds(0, half), pl.ds(half, half)

    def partial_of(quarter):
        here = pl.ds(pl.multiple_of(quarter * share, share), share)
        skipped = pl.ds(pl.multiple_of(quarter * share + HALO, HALO), share)
        attended = local[here, :] + jnp.dot(
            query[here, :], incoming[...], preferred_element_type=jnp.float32
        )
        mean_square = jnp.mean(attended * attended, axis=1, keepdims=True)
        gate_values = gate[skipped, :].astype(jnp.float32)
        gated = (
            attended
            * lax.rsqrt(mean_square + EPS_HEAD)
            * head_gain_ref[...]
            * (gate_values * jax.nn.sigmoid(gate_values))
        ).astype(jnp.bfloat16)
        return jnp.dot(gated, w_out[...], preferred_element_type=jnp.float32).astype(jnp.bfloat16)

    def move(src, dst, to, index, recv):
        return pltpu.make_async_remote_copy(
            src_ref=src,
            dst_ref=dst,
            send_sem=send_sum.at[index],
            recv_sem=recv,
            device_id={"tensor": to},
            device_id_type=MESH,
        )

    moves = [
        move(to_far.at[lower], relay_right, left, 0, recv_relay.at[0]),
        move(to_far.at[upper_half], relay_left, right, 1, recv_relay.at[1]),
        move(to_left.at[upper_half], sum_right.at[upper_half], left, 2, recv_sum.at[0]),
        move(to_right.at[lower], sum_left.at[lower], right, 3, recv_sum.at[1]),
        move(to_left.at[lower], sum_right.at[lower], left, 4, recv_sum.at[2]),
        move(to_right.at[upper_half], sum_left.at[upper_half], right, 5, recv_sum.at[3]),
    ]
    whole(back, n - 1, recv_sem.at[4])
    to_far[...] = partial_of(far)
    moves[0].start()
    moves[1].start()
    to_left[...] = partial_of(left)
    moves[2].start()
    to_right[...] = partial_of(right)
    moves[3].start()
    moves[0].wait_recv()
    to_left[lower, :] = (
        to_left[lower, :].astype(jnp.float32) + relay_right[...].astype(jnp.float32)
    ).astype(jnp.bfloat16)
    moves[4].start()
    moves[1].wait_recv()
    to_right[upper_half, :] = (
        to_right[upper_half, :].astype(jnp.float32) + relay_left[...].astype(jnp.float32)
    ).astype(jnp.bfloat16)
    moves[5].start()

    if levels > 1:
        whole(all_finals, levels - 1, recv_sem.at[5])

    def hand_states(hop, _):
        other = lax.rem(member + hop, group)
        pick_states(other)

        @pl.when(hop > 0)
        def _():
            handed_to(other).start()

        return 0

    lax.fori_loop(0, group, hand_states, 0)
    owned[mine] = handed[member]

    for copy in moves[:2]:
        copy.wait_send()
    to_far[...] = partial_of(x)
    whole(owned_edges, group - 1, recv_sem.at[3])
    total = owned_edges[0].astype(jnp.float32)
    for other in range(1, group):
        total = total + owned_edges[other].astype(jnp.float32)
    owned_edge_ref[...] = total.astype(jnp.bfloat16)
    whole(handed, group - 1, recv_sem.at[6])
    owned_ref[...] = owned[...]
    for copy in moves[2:]:
        copy.wait_recv()
    row_of = x * share + lax.broadcasted_iota(jnp.int32, (share, 1), 0)
    summed = (
        to_far[...].astype(jnp.float32)
        + sum_right[...].astype(jnp.float32)
        + sum_left[...].astype(jnp.float32)
    )
    live = live_rows_of(me, ends, fills_ref, local.shape[0])
    mixed_ref[...] = jnp.where(row_of < live, summed, 0.0).astype(jnp.bfloat16)
    for copy in moves[2:]:
        copy.wait_send()
    whole(messages, n - 1, send_sem.at[0])
    whole(parts, n - 1, send_sem.at[1])
    whole(back, n - 1, send_sem.at[4])
    whole(owned_edges, group - 1, send_sem.at[3])
    whole(handed, group - 1, send_sem.at[6])
    if levels > 1:
        whole(edges, levels - 1, send_sem.at[2])
        whole(all_finals, levels - 1, send_sem.at[5])


def handoff(
    spans,
    fills,
    wanted,
    state,
    decay,
    edge,
    head_gain,
    local_out,
    query_decayed,
    gate_values,
    w_out,
):
    n = lax.axis_size("seq")
    group = 8 if n >= 64 else 4
    levels = n // group
    keys, values = state.shape
    slots, prompts = wanted.shape[0], spans.shape[0]
    lane_blocks = values // 128
    rows = keys * lane_blocks // n
    share = local_out.shape[0] // lax.axis_size("tensor")
    width = w_out.shape[1]
    wide = max(rows, 128)
    vmem = pl.BlockSpec(memory_space=pltpu.VMEM)
    smem = pl.BlockSpec(memory_space=pltpu.SMEM)
    half = jnp.bfloat16
    owned_shape = (slots, levels, group // lane_blocks, rows, values)
    return pl.pallas_call(
        functools.partial(handoff_kernel, n, group, rows),
        out_shape=(
            jax.ShapeDtypeStruct((share, width), half),
            jax.ShapeDtypeStruct(owned_shape, half),
            jax.ShapeDtypeStruct((slots,) + edge.shape, half),
        ),
        in_specs=[smem] * 3 + [vmem] * 8,
        out_specs=(vmem,) * 3,
        scratch_shapes=[
            pltpu.VMEM((keys // wide, 1, wide + 128 * slots), jnp.float32),
            pltpu.VMEM((n, rows, 128), half),
            pltpu.VMEM((n, 1, wide + 128 * slots), jnp.float32),
            pltpu.VMEM((n, rows, 128), jnp.float32),
            pltpu.VMEM((n, rows, 128), half),
            pltpu.VMEM((keys, values), half),
            pltpu.VMEM((prompts, rows, 128), half),
            pltpu.VMEM((levels, prompts, rows, 128), half),
            pltpu.VMEM((group, slots, levels, rows, 128), half),
            pltpu.VMEM(owned_shape, half),
            pltpu.VMEM((levels,) + edge.shape, half),
            pltpu.VMEM((group, slots) + edge.shape, half),
            pltpu.VMEM((group, slots) + edge.shape, half),
        ]
        + [pltpu.VMEM((share, width), half)] * 3
        + [pltpu.VMEM((share // 2, width), half)] * 2
        + [pltpu.VMEM((share, width), half)] * 2
        + [
            pltpu.SemaphoreType.DMA((7,)),
            pltpu.SemaphoreType.DMA((7,)),
            pltpu.SemaphoreType.DMA((6,)),
            pltpu.SemaphoreType.DMA((2,)),
            pltpu.SemaphoreType.DMA((4,)),
        ],
        compiler_params=pltpu.CompilerParams(
            collective_id=0, has_side_effects=True, vmem_limit_bytes=24 * 1024 * 1024
        ),
        name="state_handoff",
    )(
        spans,
        fills,
        wanted,
        state,
        decay,
        edge,
        head_gain.reshape(1, -1),
        local_out,
        query_decayed,
        gate_values,
        w_out,
    )


def local_kernel(
    spans_ref,
    fills_ref,
    projected_ref,
    low_rank_ref,
    gate_up_wide_ref,
    gate_bias_ref,
    conv_ref,
    out_ref,
    query_ref,
    state_ref,
    decay_ref,
    edge_ref,
    state,
    offset,
    gate_up_ref,
):
    live = live_rows_of(
        lax.axis_index("seq"), prompt_edges(spans_ref), fills_ref, out_ref.shape[0]
    )
    for rank in range(gate_up_ref.shape[0]):
        gate_up_ref[rank : rank + 1, :] = gate_up_wide_ref[rank]
    rows = out_ref.shape[0]
    keys, values = state.shape
    halo = projected_ref.shape[0] - rows
    taps = conv_ref.shape[0]
    state[...] = jnp.zeros_like(state)
    offset[...] = jnp.zeros_like(offset)
    row_of = lax.broadcasted_iota(jnp.int32, (STRETCH, 1), 0)
    at_row = lax.broadcasted_iota(jnp.int32, (STRETCH, STRETCH), 0)
    at_col = lax.broadcasted_iota(jnp.int32, (STRETCH, STRETCH), 1)
    lower = (at_row >= at_col).astype(jnp.float32)
    ones = jnp.ones((STRETCH, 128), jnp.float32)

    def contract(a, b, dims, precision=None):
        return lax.dot_general(
            a, b, (dims, ((), ())), precision=precision, preferred_element_type=jnp.float32
        )

    def one_block(block, _):
        base = pl.multiple_of(block * STRETCH, STRETCH)
        here = pl.ds(base, STRETCH)
        window = projected_ref[pl.ds(base, STRETCH + halo), :].astype(jnp.float32)
        total = jnp.zeros((STRETCH, window.shape[1]), jnp.float32)
        for tap in range(taps):
            first = halo - taps + 1 + tap
            total = total + conv_ref[tap] * window[first : first + STRETCH]
        activated = (total * jax.nn.sigmoid(total)).astype(jnp.bfloat16)
        valid = base + row_of < live
        query = activated[:, :keys].astype(jnp.float32) * keys ** (-0.5)
        key = jnp.where(valid, activated[:, keys : 2 * keys].astype(jnp.float32), 0.0)
        value = activated[:, 2 * keys :]
        logits = contract(
            low_rank_ref[pl.ds(base + halo, STRETCH), :], gate_up_ref[...], ((1,), (0,)), EXACT_MATMUL
        ) + gate_bias_ref[...]
        log_decay = (jnp.minimum(logits, 0.0) - jnp.log1p(jnp.exp(-jnp.abs(logits)))) / 16.0
        log_decay = jnp.where(valid, log_decay, 0.0)
        running = contract(lower, log_decay, ((1,), (0,)), EXACT_MATMUL)
        closing = running[STRETCH - 1 : STRETCH]
        closing_column = contract(log_decay, ones, ((0,), (0,)), EXACT_MATMUL)

        scores = jnp.zeros((STRETCH, STRETCH), jnp.float32)
        half = STRETCH // 2
        while half >= 8:
            pair = 2 * half
            pieces = []
            for first in range(0, STRETCH, pair):
                middle = running[first + half - 1 : first + half]
                pieces.append(jnp.broadcast_to(middle, (pair, keys)))
            middle = pieces[0] if len(pieces) == 1 else jnp.concatenate(pieces, axis=0)
            factor = jnp.exp(-jnp.abs(running - middle))
            second = row_of % pair >= half
            left = jnp.where(second, query * factor, 0.0).astype(jnp.bfloat16)
            right = jnp.where(second, 0.0, key * factor).astype(jnp.bfloat16)
            part = contract(left, right, ((1,), (1,)))
            scores = scores + jnp.where(at_row // pair == at_col // pair, part, 0.0)
            half //= 2
        for shift in range(8):
            if shift:
                moved_key = pltpu.roll(key, shift, 0)
                moved_sum = pltpu.roll(running, shift, 0)
                product = query * moved_key * jnp.exp(jnp.minimum(running - moved_sum, 0.0))
            else:
                product = query * key
            summed = jnp.sum(product, axis=1, keepdims=True)
            chosen = (at_col == at_row - shift) & (at_row % 8 >= shift)
            scores = scores + jnp.where(chosen, summed, 0.0)

        decayed = (query * jnp.exp(running)).astype(jnp.bfloat16)
        weighted = (key * jnp.exp(closing - running)).astype(jnp.bfloat16)
        query_ref[here, :] = (query * jnp.exp(running + offset[...])).astype(jnp.bfloat16)
        before = state[...]
        out_ref[here, :] = contract(
            scores.astype(jnp.bfloat16), value, ((1,), (0,))
        ) + contract(decayed, before.astype(jnp.bfloat16), ((1,), (0,)))
        factor = jnp.exp(closing_column)
        factor = jnp.concatenate([factor] * (values // 128), axis=1)
        state[...] = factor * before + contract(weighted, value, ((0,), (0,)))
        offset[...] = offset[...] + closing
        return 0

    lax.fori_loop(0, rows // STRETCH, one_block, 0)
    state_ref[...] = state[...].astype(jnp.bfloat16)
    decay_ref[...] = jnp.exp(offset[...])
    first = live + halo - taps + 1
    base = pl.multiple_of(jnp.minimum(first // 16 * 16, rows + halo - 32), 16)
    window = projected_ref[pl.ds(base, 32), :]
    wanted = lax.broadcasted_iota(jnp.int32, (8, 32), 0) + (first - base)
    here = lax.broadcasted_iota(jnp.int32, (8, 32), 1)
    chosen = (wanted == here).astype(jnp.bfloat16)
    edge_ref[...] = contract(chosen, window, ((1,), (0,))).astype(jnp.bfloat16)


def local_blocks(spans, fills, projected, low_rank, gate_up, gate_bias, conv_weight, values):
    rows = low_rank.shape[0] - HALO
    keys = gate_up.shape[2]
    vmem = pl.BlockSpec(memory_space=pltpu.VMEM)
    smem = pl.BlockSpec(memory_space=pltpu.SMEM)
    return pl.pallas_call(
        local_kernel,
        out_shape=(
            jax.ShapeDtypeStruct((rows, values), jnp.float32),
            jax.ShapeDtypeStruct((rows, keys), jnp.bfloat16),
            jax.ShapeDtypeStruct((keys, values), jnp.bfloat16),
            jax.ShapeDtypeStruct((1, keys), jnp.float32),
            jax.ShapeDtypeStruct((8, projected.shape[1]), jnp.bfloat16),
        ),
        in_specs=[smem, smem] + [vmem] * 5,
        out_specs=(vmem,) * 5,
        scratch_shapes=[
            pltpu.VMEM((keys, values), jnp.float32),
            pltpu.VMEM((1, keys), jnp.float32),
            pltpu.VMEM((gate_up.shape[0], keys), jnp.float32),
        ],
        compiler_params=pltpu.CompilerParams(vmem_limit_bytes=20 * 1024 * 1024),
        name="local_blocks",
    )(spans, fills, projected, low_rank, gate_up, gate_bias, conv_weight)


def body(
    tokens,
    norm_gain,
    w_qkv,
    w_gate_out,
    gate_down,
    gate_up,
    gate_bias,
    conv_weight,
    head_gain,
    w_out,
    spans,
    fills,
    request_prompt,
):
    model_width, local_heads, width_qkv = w_qkv.shape
    value_width = head_gain.shape[0]
    key_width = gate_up.shape[2]
    taps = conv_weight.shape[0]
    slot_count = request_prompt.shape[0]
    flat_qkv = w_qkv.reshape(model_width, local_heads * width_qkv)
    extended, gate_values, low_rank = project(
        spans, tokens, norm_gain, flat_qkv, w_gate_out, gate_down
    )
    local_out, query_decayed, local_state, decay, edge = local_blocks(
        spans, fills, extended, low_rank, gate_up, gate_bias, conv_weight, value_width
    )
    mixed, owned_state, owned_edge = handoff(
        spans,
        fills,
        request_prompt,
        local_state,
        decay,
        edge,
        head_gain,
        local_out,
        query_decayed,
        gate_values,
        w_out,
    )
    owner_state = owned_state.reshape(slot_count, local_heads, key_width, value_width).astype(
        jnp.float32
    )
    owner_edge = owned_edge[:, : taps - 1].reshape(slot_count, taps - 1, local_heads, width_qkv)
    return (mixed, owner_state, owner_edge)


def solution(mesh):
    return jax.shard_map(
        body,
        mesh=mesh,
        in_specs=(
            P("seq", "tensor"),
            P(),
            P(None, "tensor", None),
            P(None, "tensor"),
            P(),
            P(None, "tensor", None),
            P("tensor", None),
            P(None, "tensor", None),
            P(),
            P("tensor", None),
            P(),
            P(),
            P("seq"),
        ),
        out_specs=(
            P(("seq", "tensor"), None),
            P("seq", "tensor", None, None),
            P("seq", None, "tensor", None),
        ),
        check_vma=False,
    )
```
